32 devices in a mesh: group: 2 (over x), lat: 16 (over z, y, core).
Axes of the slice: x: 2, y: 2, z: 4, core: 2. Of those that a mesh axis runs over, the one named last changes fastest.
Arguments:
- currents: float32 [16, 2, 512, 512], P('group', None, 'lat'), parts along dimension 0, may hold values from -6 to 6
- green: float32 [16, 8, 2, 1024, 1024], P('group', None, None, 'lat'), parts along dimension 0, may hold values from -5 to 5
- section_map: int32 [16], P('group'), parts along dimension 0, may hold values from 0 to 7
- offsets: int32 [16], P('group'), parts along dimension 0, may hold values from 0 to 512
Outputs:
- fields: float32 [16, 2, 512, 512], P('group', None, 'lat'), parts along dimension 0
The draws below stay inside these ranges and needn't reach their ends.
There are 2 independent parts, one for each index of `group`. The reference program is written for one: setup_inputs(seed, part) draws one part's arguments, and reference() takes and returns one part's arrays. A program takes and returns all parts, laid end to end along the dimension named above; each array names one. Nothing has to cross between parts.
All inputs are finite; a program needn't handle non-finite values.
Results may differ from the reference program's by a relative error of at most 0.0003.
Values sent between devices are 32-bit elements; how exact they have to be, the bound alone decides.
No kernel may reach another device: no remote copies, remote signals or barrier semaphores. Data moves between devices by JAX's collectives and lax.ppermute only.
A program may use at most 128 MiB of HBM per device.

```python
import jax
import jax.numpy as jnp
from jax import lax

N = 512
PADDED = 1024
DEPTHS = 8
SECTIONS = 8


def place_ends(result, rng, smallest, top_value):
    spot = [jax.random.randint(jax.random.fold_in(rng, axis), (), 0, length) for axis, length in enumerate(result.shape)]
    main_axis = result.shape.index(max(result.shape))
    next_to = spot[:main_axis] + [(spot[main_axis] + 1) % result.shape[main_axis]] + spot[main_axis + 1:]
    return result.at[tuple(spot)].set(smallest).at[tuple(next_to)].set(top_value)


def steps_of(key, dims, split, low, largest):
    gain, own = 1.0, jax.random.fold_in(key, 6)
    for axis_at, parts in split:
        steps = jnp.exp(jax.random.uniform(jax.random.fold_in(own, axis_at), (parts,), jnp.float32, low / len(split), largest / len(split)))
        gain = gain * jnp.repeat(steps, dims[axis_at] // parts).reshape([-1 if axis == axis_at else 1 for axis in range(len(dims))])
    return gain


def centred(key, shape, scale, reach, split=(), kind=jnp.bfloat16):
    entries = jax.random.normal(key, shape, jnp.float32) * scale
    if len(split) > 0:
        entries = steps_of(key, shape, split, -0.22, 0.18) * entries
    return jnp.clip(entries, min=-reach, max=reach).astype(kind)


def setup_inputs(seed: int = 0, part: int = 0) -> dict:
    streams_of = jax.random.split(jax.random.key(seed), 5)
    own_keys = jax.random.split(jax.random.fold_in(streams_of[4], part), 5)
    currents = centred(own_keys[0], (DEPTHS, 2, N, N), 1.0, 6.0, ((2, 16),), jnp.float32)
    green = centred(own_keys[1], (SECTIONS, SECTIONS, 2, PADDED, PADDED), 0.35, 5.0, ((3, 16),), jnp.float32)
    section_map = place_ends(jax.random.randint(own_keys[2], (DEPTHS,), 0, SECTIONS), jax.random.fold_in(own_keys[2], 1), 0, SECTIONS - 1).astype(jnp.int32)
    offsets = place_ends(jax.random.randint(own_keys[3], (DEPTHS,), 0, N + 1), jax.random.fold_in(own_keys[3], 1), 0, N).astype(jnp.int32)
    return {"currents": currents, "green": green, "section_map": section_map, "offsets": offsets}


def embed_plane(plane, offset):
    blank = jnp.zeros((2 * N, 2 * N), plane.dtype)
    return lax.dynamic_update_slice(blank, plane, (jnp.int32(0), offset.astype(jnp.int32)))


def crop_plane(plane, offset):
    return lax.dynamic_slice(plane, (jnp.int32(0), offset.astype(jnp.int32)), (N, N))


def reference(currents, green, section_map, offsets):
    planes = lax.complex(currents[:, 0], currents[:, 1])
    spectrum = jnp.fft.fft2(jax.vmap(embed_plane)(planes, offsets))
    onehot = (section_map[:, None] == jnp.arange(SECTIONS, dtype=jnp.int32)[None, :]).astype(currents.dtype)
    section_spec = jnp.einsum("js,jab->sab", onehot.astype(spectrum.dtype), spectrum)
    green_complex = lax.complex(green[:, :, 0], green[:, :, 1])
    coupled = jnp.einsum("tsqk,skq->tkq", green_complex, section_spec)
    per_depth = jnp.einsum("js,sab->jab", onehot.astype(coupled.dtype), coupled)
    fields = jax.vmap(crop_plane)(jnp.fft.ifft2(per_depth), offsets)
    return jnp.stack([jnp.real(fields), jnp.imag(fields)], axis=1).astype(jnp.float32)
```

```python
import functools
import math

import jax
import jax.numpy as jnp
import numpy as np
from jax import lax
from jax.experimental import pallas as pl
from jax.experimental.pallas import tpu as pltpu
from jax.sharding import PartitionSpec as P

RADIX = 4
LANES = 128
FINE = 32
F32 = jnp.float32
BF16 = jnp.bfloat16


def dft_table(n_in, n_out, period, sign_value):
    row_ids = lax.iota(jnp.int32, n_in)
    col_ids = lax.iota(jnp.int32, n_out)
    angles = (
        2.0 * math.pi / period * (row_ids[:, None] * col_ids[None, :] % period).astype(jnp.float32)
    )
    cosine = jnp.cos(angles)
    sine_part = sign_value * jnp.sin(angles)
    return jnp.stack(
        [jnp.stack([cosine, sine_part], axis=1), jnp.stack([-sine_part, cosine], axis=1)], axis=0
    )


def phases(offsets, period, sign_value):
    col_ids = lax.iota(jnp.int32, period)
    angles = (
        2.0 * math.pi / period * (offsets[:, None] * col_ids[None, :] % period).astype(jnp.float32)
    )
    return (jnp.cos(angles)[:, None, :], sign_value * jnp.sin(angles)[:, None, :])


def rotate(planes, cosine, sine_part):
    real_part = planes[:, 0] * cosine - planes[:, 1] * sine_part
    imag_part = planes[:, 0] * sine_part + planes[:, 1] * cosine
    return jnp.stack([real_part, imag_part], axis=1)


def plain_per_device(currents, green, section_map, offsets):
    highest = lax.Precision.HIGHEST
    plane_width = currents.shape[3]
    padded = 2 * plane_width
    sections = green.shape[0]
    forward = dft_table(plane_width, padded, padded, -1.0)
    inverse = dft_table(padded, plane_width, padded, 1.0)
    onehot = (section_map[:, None] == lax.iota(jnp.int32, sections)[None, :]).astype(jnp.float32)
    spec_y = jnp.einsum("jcxy,cydk->jdxk", currents, forward, precision=highest)
    cos_fwd, sin_fwd = phases(offsets, padded, -1.0)
    shifted = jnp.transpose(rotate(spec_y, cos_fwd, sin_fwd), (0, 2, 1, 3))
    grouped = jnp.einsum("js,jxdk->sxdk", onehot, shifted, precision=highest)
    spectra = jnp.einsum(
        "mxcq,cxdk->mdqk",
        lax.all_to_all(grouped, "lat", split_axis=3, concat_axis=1, tiled=True),
        forward,
        precision=highest,
    )
    green_real = green[:, :, 0]
    green_imag = green[:, :, 1]
    out_real = jnp.einsum(
        "tsqk,sqk->tqk", green_real, spectra[:, 0], precision=highest
    ) - jnp.einsum("tsqk,sqk->tqk", green_imag, spectra[:, 1], precision=highest)
    out_imag = jnp.einsum(
        "tsqk,sqk->tqk", green_real, spectra[:, 1], precision=highest
    ) + jnp.einsum("tsqk,sqk->tqk", green_imag, spectra[:, 0], precision=highest)
    coupled = jnp.stack([out_real, out_imag], axis=1)
    returned = lax.all_to_all(
        jnp.einsum("mcqk,ckdx->mdxq", coupled, inverse, precision=highest),
        "lat",
        split_axis=2,
        concat_axis=3,
        tiled=True,
    )
    per_depth = jnp.einsum("js,sdxq->jdxq", onehot, returned, precision=highest)
    cos_back, sin_back = phases(offsets, padded, 1.0)
    turned = rotate(per_depth, cos_back, sin_back)
    result = jnp.einsum("jcxk,ckdy->jdxy", turned, inverse, precision=highest)
    return result * (1.0 / (padded * padded))


def split_np(table):
    high = table.astype(BF16)
    low = (table - high.astype(np.float64)).astype(BF16)
    return high, low


def unit(products, period):
    angles = (2.0 * math.pi / period) * (products % period).astype(np.float64)
    return np.cos(angles), np.sin(angles)


def tables(width):
    padded = 2 * width
    inner = padded // RADIX
    taps = width // RADIX
    cosine, sine = unit(np.arange(taps)[:, None] * np.arange(inner)[None, :], inner)
    weights = np.concatenate(
        [np.concatenate([cosine, -sine], axis=1), np.concatenate([sine, cosine], axis=1)], axis=0
    )
    forward = split_np(weights)
    inverse = split_np(np.ascontiguousarray(weights.T) / (padded * 1.0))
    cosine, sine = unit(np.arange(8)[:, None] * np.arange(inner)[None, :], padded)
    twiddle = np.stack([cosine, -sine]).astype(np.float32)
    lanes = np.arange(padded).reshape(1, padded // LANES, LANES)
    cosine, sine = unit(np.arange(FINE)[:, None, None] * lanes, padded)
    fine = np.stack([cosine, -sine]).astype(np.float32)
    cosine, sine = unit(FINE * np.arange(width // FINE + 1)[:, None, None] * lanes, padded)
    coarse = np.stack([cosine, -sine]).astype(np.float32)
    return forward, inverse, twiddle, fine, coarse


def cmul(a, b):
    return a[0] * b[0] - a[1] * b[1], a[0] * b[1] + a[1] * b[0]


def cadd(a, b):
    return a[0] + b[0], a[1] + b[1]


def csub(a, b):
    return a[0] - b[0], a[1] - b[1]


def butterfly(v, turn):
    even, odd = cadd(v[0], v[2]), csub(v[0], v[2])
    cross, diff = cadd(v[1], v[3]), csub(v[1], v[3])
    spun = (-turn * diff[1], turn * diff[0])
    return cadd(even, cross), cadd(odd, spun), csub(even, cross), csub(odd, spun)


def split(value):
    high = value.astype(BF16)
    return high, (value - high.astype(F32)).astype(BF16)


def dot3(value, high_table, low_table):
    high, low = split(value)
    dot = functools.partial(jnp.dot, preferred_element_type=F32)
    return dot(high, high_table) + (dot(high, low_table) + dot(low, high_table))


def phase_rows(fine_ref, coarse_ref, offset):
    fine_id = offset % FINE
    coarse_id = offset // FINE
    return cmul(
        tuple(fine_ref[d, fine_id] for d in range(2)),
        tuple(coarse_ref[d, coarse_id] for d in range(2)),
    )


def plan_kernel(map_ref, plan_ref, *, depths, sections):
    count = jnp.int32(0)
    for u in range(sections):
        plan_ref[1 + u] = jnp.int32(0)
    ids = [map_ref[j] for j in range(depths)]
    for s in range(sections):
        used = jnp.int32(0)
        for j in range(depths):
            used = jnp.maximum(used, (ids[j] == s).astype(jnp.int32))

        @pl.when(used > 0)
        def _(s=s, count=count):
            plan_ref[1 + count] = jnp.int32(s)
            for j in range(depths):
                @pl.when(ids[j] == s)
                def _(j=j):
                    plan_ref[1 + sections + j] = count

        count = count + used
    plan_ref[0] = count


def rows_kernel(
    plan_ref, off_ref, cur_ref, wh_ref, wl_ref, tw_ref, fine_ref, coarse_ref, out_ref,
    turned_ref, mid_ref, acc_ref, *, slots, sections, batch
):
    depths, _, rows, width = cur_ref.shape
    padded = 2 * width
    inner = padded // RADIX
    taps = width // RADIX
    tall = batch * rows
    acc_ref[...] = jnp.zeros(acc_ref.shape, F32)

    @pl.loop(0, depths // batch)
    def _(g):
        for c in range(2):
            block = cur_ref[pl.ds(g * batch, batch), c].reshape(tall, width)
            turned_ref[c] = block.T
        parts = []
        for r in range(RADIX):
            parts.append(
                jnp.concatenate(
                    [turned_ref[c, pl.ds(r, taps, stride=RADIX), :].T for c in range(2)], axis=1
                )
            )
        mid_ref[...] = dot3(jnp.concatenate(parts, axis=0), wh_ref[...], wl_ref[...])

        @pl.loop(0, batch)
        def _(jj):
            j = g * batch + jj
            turn = phase_rows(fine_ref, coarse_ref, off_ref[j])
            slot = plan_ref[1 + sections + j]
            for k in range(0, inner, LANES):
                values = []
                for r in range(RADIX):
                    at = pl.ds(r * tall + jj * rows, rows)
                    value = tuple(mid_ref[at, d * inner + k : d * inner + k + LANES] for d in range(2))
                    if r > 0:
                        value = cmul(value, tuple(tw_ref[d, r : r + 1, k : k + LANES] for d in range(2)))
                    values.append(value)
                for q, value in enumerate(butterfly(values, -1.0)):
                    lanes = slice(q * inner + k, q * inner + k + LANES)
                    b = (q * inner + k) // LANES
                    value = cmul(value, (turn[0][b : b + 1], turn[1][b : b + 1]))
                    for d in range(2):
                        acc_ref[slot, d, :, lanes] += value[d]

    half = LANES // 2
    low = lax.broadcasted_iota(jnp.int32, (rows, LANES), 1) < half

    @pl.loop(0, slots)
    def _(u):
        for b in range(padded // LANES):
            lanes = slice(b * LANES, (b + 1) * LANES)
            re = acc_ref[u, 0, :, lanes]
            im = acc_ref[u, 1, :, lanes]
            out_ref[2 * b, u] = jnp.where(low, re, pltpu.roll(im, half, 1))
            out_ref[2 * b + 1, u] = jnp.where(low, pltpu.roll(re, half, 1), im)


def couple_kernel(
    plan_ref, in_ref, wh_ref, wl_ref, vh_ref, vl_ref, tw_ref, green_ref, out_ref,
    green_buf, spec_ref, mid_ref, lhs_ref, sems, *, slots
):
    parts, _, rows, _ = in_ref.shape
    columns, padded = green_buf.shape[3], green_buf.shape[4]
    inner = padded // RADIX
    taps = parts * rows // RADIX
    own = rows // RADIX

    def fetch(t, s):
        return pltpu.make_async_copy(
            green_ref.at[plan_ref[1 + t], plan_ref[1 + s]], green_buf.at[t, s], sems.at[t, s]
        )

    for t in range(slots):
        for s in range(slots):
            fetch(t, s).start()

    tiles = [(a, k) for a in range(0, columns, 8) for k in range(0, inner, LANES)]

    @pl.loop(0, slots)
    def _(u):
        blocks = []
        for r in range(RADIX):
            tall = jnp.concatenate(
                [in_ref[p, u, pl.ds(r, own, stride=RADIX), :] for p in range(parts)], axis=0
            ).T
            blocks.append(jnp.concatenate([tall[:columns], tall[columns:]], axis=1))
        mid_ref[...] = dot3(jnp.concatenate(blocks, axis=0), wh_ref[...], wl_ref[...])
        for a, k in tiles:
            values = []
            for r in range(RADIX):
                at = slice(r * columns + a, r * columns + a + 8)
                value = tuple(mid_ref[at, d * inner + k : d * inner + k + LANES] for d in range(2))
                if r > 0:
                    value = cmul(value, tuple(tw_ref[d, r : r + 1, k : k + LANES] for d in range(2)))
                values.append(value)
            for q, value in enumerate(butterfly(values, -1.0)):
                for d in range(2):
                    spec_ref[u, d, a : a + 8, q * inner + k : q * inner + k + LANES] = value[d]

    @pl.loop(0, slots)
    def _(t):
        for s in range(slots):
            fetch(t, s).wait()

        @pl.loop(0, columns // 8)
        def _(a8):
            at = pl.ds(pl.multiple_of(a8 * 8, 8), 8)
            for k in range(0, inner, LANES):
                coupled = []
                for q in range(RADIX):
                    lanes = slice(q * inner + k, q * inner + k + LANES)
                    total = None
                    for s in range(slots):
                        term = cmul(
                            tuple(green_buf[t, s, d, at, lanes] for d in range(2)),
                            tuple(spec_ref[s, d, at, lanes] for d in range(2)),
                        )
                        total = term if total is None else cadd(total, term)
                    coupled.append(total)
                for r, value in enumerate(butterfly(coupled, 1.0)):
                    if r > 0:
                        back = (tw_ref[0, r : r + 1, k : k + LANES], -tw_ref[1, r : r + 1, k : k + LANES])
                        value = cmul(value, back)
                    for d in range(2):
                        here = pl.ds(pl.multiple_of(r * columns + a8 * 8, 8), 8)
                        lhs_ref[here, d * inner + k : d * inner + k + LANES] = value[d]

        result = dot3(lhs_ref[...], vh_ref[...], vl_ref[...])
        for r in range(RADIX):
            block = result[r * columns : (r + 1) * columns]
            tall = jnp.concatenate([block[:, :taps], block[:, taps:]], axis=0).T
            for p in range(parts):
                out_ref[p, t, pl.ds(r, own, stride=RADIX), :] = tall[p * own : (p + 1) * own]


def fields_kernel(
    plan_ref, off_ref, in_ref, vh_ref, vl_ref, tw_ref, fine_ref, coarse_ref, out_ref,
    spec_ref, lhs_ref, turned_ref, *, slots, sections, batch
):
    depths, _, rows, width = out_ref.shape
    padded = 2 * width
    inner = padded // RADIX
    taps = width // RADIX
    tall = batch * rows
    half = LANES // 2
    low = lax.broadcasted_iota(jnp.int32, (rows, LANES), 1) < half

    @pl.loop(0, slots)
    def _(u):
        for b in range(padded // LANES):
            lanes = slice(b * LANES, (b + 1) * LANES)
            first = in_ref[2 * b, u]
            second = in_ref[2 * b + 1, u]
            spec_ref[u, 0, :, lanes] = jnp.where(low, first, pltpu.roll(second, half, 1))
            spec_ref[u, 1, :, lanes] = jnp.where(low, pltpu.roll(first, half, 1), second)

    @pl.loop(0, depths // batch)
    def _(g):
        @pl.loop(0, batch)
        def _(jj):
            j = g * batch + jj
            turn = phase_rows(fine_ref, coarse_ref, off_ref[j])
            slot = plan_ref[1 + sections + j]
            for k in range(0, inner, LANES):
                values = []
                for q in range(RADIX):
                    lanes = slice(q * inner + k, q * inner + k + LANES)
                    b = (q * inner + k) // LANES
                    value = tuple(spec_ref[slot, d, :, lanes] for d in range(2))
                    values.append(cmul(value, (turn[0][b : b + 1], -turn[1][b : b + 1])))
                for r, value in enumerate(butterfly(values, 1.0)):
                    if r > 0:
                        back = (tw_ref[0, r : r + 1, k : k + LANES], -tw_ref[1, r : r + 1, k : k + LANES])
                        value = cmul(value, back)
                    for d in range(2):
                        here = pl.ds(r * tall + jj * rows, rows)
                        lhs_ref[here, d * inner + k : d * inner + k + LANES] = value[d]

        result = dot3(lhs_ref[...], vh_ref[...], vl_ref[...])
        for d in range(2):
            for r in range(RADIX):
                block = result[r * tall : (r + 1) * tall, d * taps : (d + 1) * taps]
                turned_ref[d, pl.ds(r, taps, stride=RADIX), :] = block.T
            out_ref[pl.ds(g * batch, batch), d] = turned_ref[d].T.reshape(batch, rows, width)


def vmem():
    return pl.BlockSpec(memory_space=pltpu.VMEM)


def smem():
    return pl.BlockSpec(memory_space=pltpu.SMEM)


PARAMS = pltpu.CompilerParams(vmem_limit_bytes=56 * 1024 * 1024)


def per_device(currents, green, section_map, offsets, *, parts):
    depths, _, rows, width = currents.shape
    sections = green.shape[0]
    columns = green.shape[3]
    padded = 2 * width
    inner = padded // RADIX
    taps = width // RADIX
    batch = LANES // rows
    (wh, wl), (vh, vl), twiddle, fine, coarse = (
        jax.tree.map(jnp.asarray, entry) for entry in tables(width)
    )
    plan = pl.pallas_call(
        functools.partial(plan_kernel, depths=depths, sections=sections),
        out_shape=jax.ShapeDtypeStruct((1 + sections + depths,), jnp.int32),
        in_specs=[smem()],
        out_specs=smem(),
        name="plan",
    )(section_map)

    def run(slots, plan, offsets, currents, green, wh, wl, vh, vl, twiddle, fine, coarse):
        blocks = jax.ShapeDtypeStruct((parts, slots, rows, LANES), F32)
        sent = pl.pallas_call(
            functools.partial(rows_kernel, slots=slots, sections=sections, batch=batch),
            out_shape=blocks,
            in_specs=[smem(), smem()] + [vmem()] * 6,
            out_specs=vmem(),
            scratch_shapes=[
                pltpu.VMEM((2, width, LANES), F32),
                pltpu.VMEM((RADIX * LANES, 2 * inner), F32),
                pltpu.VMEM((slots, 2, rows, padded), F32),
            ],
            compiler_params=PARAMS,
            name=f"rows_{slots}",
        )(plan, offsets, currents, wh, wl, twiddle, fine, coarse)
        got = lax.all_to_all(sent, "lat", 0, 0, tiled=True)
        back = pl.pallas_call(
            functools.partial(couple_kernel, slots=slots),
            out_shape=blocks,
            in_specs=[smem()] + [vmem()] * 6 + [pl.BlockSpec(memory_space=pl.ANY)],
            out_specs=vmem(),
            scratch_shapes=[
                pltpu.VMEM((slots, slots, 2, columns, padded), F32),
                pltpu.VMEM((slots, 2, columns, padded), F32),
                pltpu.VMEM((RADIX * columns, 2 * inner), F32),
                pltpu.VMEM((RADIX * columns, 2 * inner), F32),
                pltpu.SemaphoreType.DMA((slots, slots)),
            ],
            compiler_params=PARAMS,
            name=f"couple_{slots}",
        )(plan, got, wh, wl, vh, vl, twiddle, green)
        home = lax.all_to_all(back, "lat", 0, 0, tiled=True)
        return pl.pallas_call(
            functools.partial(fields_kernel, slots=slots, sections=sections, batch=batch),
            out_shape=jax.ShapeDtypeStruct(currents.shape, F32),
            in_specs=[smem(), smem()] + [vmem()] * 6,
            out_specs=vmem(),
            scratch_shapes=[
                pltpu.VMEM((slots, 2, rows, padded), F32),
                pltpu.VMEM((RADIX * LANES, 2 * inner), F32),
                pltpu.VMEM((2, width, LANES), F32),
            ],
            compiler_params=PARAMS,
            name=f"fields_{slots}",
        )(plan, offsets, home, vh, vl, twiddle, fine, coarse)

    least = max(1, min(depths, sections) // 2)
    choices = list(range(least, min(depths, sections) + 1))
    return lax.switch(
        jnp.maximum(plan[0] - least, 0),
        [functools.partial(run, slots) for slots in choices],
        plan, offsets, currents, green, wh, wl, vh, vl, twiddle, fine, coarse,
    )


def solution(mesh):
    parts = mesh.shape["lat"]

    def body(currents, green, section_map, offsets):
        depths, _, rows, width = currents.shape
        columns = green.shape[3]
        fits = (
            2 * columns == LANES
            and rows % (8 * RADIX) == 0
            and LANES % rows == 0
            and depths % (LANES // rows) == 0
            and width % (RADIX * LANES) == 0
            and columns * parts == 2 * width
        )
        if fits:
            return per_device(currents, green, section_map, offsets, parts=parts)
        return plain_per_device(currents, green, section_map, offsets)

    in_specs = (
        P("group", None, "lat", None),
        P("group", None, None, "lat", None),
        P("group"),
        P("group"),
    )
    out_specs = P("group", None, "lat", None)
    return jax.shard_map(
        body, mesh=mesh, in_specs=in_specs, out_specs=out_specs, check_vma=False
    )
```

```python
import functools
import math

import jax
import jax.numpy as jnp
import numpy as np
from jax import lax
from jax.experimental import pallas as pl
from jax.experimental.pallas import tpu as pltpu
from jax.sharding import PartitionSpec as P

RADIX = 4
LANES = 128
FINE = 32
F32 = jnp.float32
BF16 = jnp.bfloat16


def dft_table(n_in, n_out, period, sign_value):
    row_ids = lax.iota(jnp.int32, n_in)
    col_ids = lax.iota(jnp.int32, n_out)
    angles = (
        2.0 * math.pi / period * (row_ids[:, None] * col_ids[None, :] % period).astype(jnp.float32)
    )
    cosine = jnp.cos(angles)
    sine_part = sign_value * jnp.sin(angles)
    return jnp.stack(
        [jnp.stack([cosine, sine_part], axis=1), jnp.stack([-sine_part, cosine], axis=1)], axis=0
    )


def phases(offsets, period, sign_value):
    col_ids = lax.iota(jnp.int32, period)
    angles = (
        2.0 * math.pi / period * (offsets[:, None] * col_ids[None, :] % period).astype(jnp.float32)
    )
    return (jnp.cos(angles)[:, None, :], sign_value * jnp.sin(angles)[:, None, :])


def rotate(planes, cosine, sine_part):
    real_part = planes[:, 0] * cosine - planes[:, 1] * sine_part
    imag_part = planes[:, 0] * sine_part + planes[:, 1] * cosine
    return jnp.stack([real_part, imag_part], axis=1)


def plain_per_device(currents, green, section_map, offsets):
    highest = lax.Precision.HIGHEST
    plane_width = currents.shape[3]
    padded = 2 * plane_width
    sections = green.shape[0]
    forward = dft_table(plane_width, padded, padded, -1.0)
    inverse = dft_table(padded, plane_width, padded, 1.0)
    onehot = (section_map[:, None] == lax.iota(jnp.int32, sections)[None, :]).astype(jnp.float32)
    spec_y = jnp.einsum("jcxy,cydk->jdxk", currents, forward, precision=highest)
    cos_fwd, sin_fwd = phases(offsets, padded, -1.0)
    shifted = jnp.transpose(rotate(spec_y, cos_fwd, sin_fwd), (0, 2, 1, 3))
    grouped = jnp.einsum("js,jxdk->sxdk", onehot, shifted, precision=highest)
    spectra = jnp.einsum(
        "mxcq,cxdk->mdqk",
        lax.all_to_all(grouped, "lat", split_axis=3, concat_axis=1, tiled=True),
        forward,
        precision=highest,
    )
    green_real = green[:, :, 0]
    green_imag = green[:, :, 1]
    out_real = jnp.einsum(
        "tsqk,sqk->tqk", green_real, spectra[:, 0], precision=highest
    ) - jnp.einsum("tsqk,sqk->tqk", green_imag, spectra[:, 1], precision=highest)
    out_imag = jnp.einsum(
        "tsqk,sqk->tqk", green_real, spectra[:, 1], precision=highest
    ) + jnp.einsum("tsqk,sqk->tqk", green_imag, spectra[:, 0], precision=highest)
    coupled = jnp.stack([out_real, out_imag], axis=1)
    returned = lax.all_to_all(
        jnp.einsum("mcqk,ckdx->mdxq", coupled, inverse, precision=highest),
        "lat",
        split_axis=2,
        concat_axis=3,
        tiled=True,
    )
    per_depth = jnp.einsum("js,sdxq->jdxq", onehot, returned, precision=highest)
    cos_back, sin_back = phases(offsets, padded, 1.0)
    turned = rotate(per_depth, cos_back, sin_back)
    result = jnp.einsum("jcxk,ckdy->jdxy", turned, inverse, precision=highest)
    return result * (1.0 / (padded * padded))


def split_np(table):
    high = table.astype(BF16)
    low = (table - high.astype(np.float64)).astype(BF16)
    return high, low


def unit(products, period):
    angles = (2.0 * math.pi / period) * (products % period).astype(np.float64)
    return np.cos(angles), np.sin(angles)


def tables(width):
    padded = 2 * width
    inner = padded // RADIX
    taps = width // RADIX
    cosine, sine = unit(np.arange(taps)[:, None] * np.arange(inner)[None, :], inner)
    weights = np.concatenate(
        [np.concatenate([cosine, -sine], axis=1), np.concatenate([sine, cosine], axis=1)], axis=0
    )
    forward = split_np(weights)
    inverse = split_np(np.ascontiguousarray(weights.T) / (padded * 1.0))
    cosine, sine = unit(np.arange(8)[:, None] * np.arange(inner)[None, :], padded)
    twiddle = np.stack([cosine, -sine]).astype(np.float32)
    lanes = np.arange(padded).reshape(1, padded // LANES, LANES)
    cosine, sine = unit(np.arange(FINE)[:, None, None] * lanes, padded)
    fine = np.stack([cosine, -sine]).astype(np.float32)
    cosine, sine = unit(FINE * np.arange(width // FINE + 1)[:, None, None] * lanes, padded)
    coarse = np.stack([cosine, -sine]).astype(np.float32)
    return forward, inverse, twiddle, fine, coarse


def cmul(a, b):
    return a[0] * b[0] - a[1] * b[1], a[0] * b[1] + a[1] * b[0]


def cadd(a, b):
    return a[0] + b[0], a[1] + b[1]


def csub(a, b):
    return a[0] - b[0], a[1] - b[1]


def butterfly(v, turn):
    even, odd = cadd(v[0], v[2]), csub(v[0], v[2])
    cross, diff = cadd(v[1], v[3]), csub(v[1], v[3])
    spun = (-turn * diff[1], turn * diff[0])
    return cadd(even, cross), cadd(odd, spun), csub(even, cross), csub(odd, spun)


def split(value):
    high = value.astype(BF16)
    return high, (value - high.astype(F32)).astype(BF16)


def dot3(value, high_table, low_table):
    high, low = split(value)
    dot = functools.partial(jnp.dot, preferred_element_type=F32)
    return dot(high, high_table) + (dot(high, low_table) + dot(low, high_table))


def phase_rows(fine_ref, coarse_ref, offset):
    fine_id = offset % FINE
    coarse_id = offset // FINE
    return cmul(
        tuple(fine_ref[d, fine_id] for d in range(2)),
        tuple(coarse_ref[d, coarse_id] for d in range(2)),
    )


def plan_kernel(map_ref, plan_ref, *, depths, sections):
    count = jnp.int32(0)
    for u in range(sections):
        plan_ref[1 + u] = jnp.int32(0)
    ids = [map_ref[j] for j in range(depths)]
    for s in range(sections):
        used = jnp.int32(0)
        for j in range(depths):
            used = jnp.maximum(used, (ids[j] == s).astype(jnp.int32))

        @pl.when(used > 0)
        def _(s=s, count=count):
            plan_ref[1 + count] = jnp.int32(s)
            for j in range(depths):
                @pl.when(ids[j] == s)
                def _(j=j):
                    plan_ref[1 + sections + j] = count

        count = count + used
    plan_ref[0] = count


def hop_order(parts):
    quarter = max(parts // 4, 1)
    far = [d for low in range(quarter) for d in (2 * quarter + low, 3 * quarter + low) if d < parts]
    near = [d for d in range(quarter, 2 * quarter)] + [d for d in range(quarter - 1, 0, -1)]
    return (0, *far[:4], *near[:1], *far[4:], *near[1:])


def copy_all(copies):
    for copy in copies:
        copy.start()
    return copies


def wait_all(copies):
    for copy in copies:
        copy.wait()


def rows_kernel(
    plan_ref, off_ref, cur_ref, wh_hbm, wl_hbm, tw_hbm, fine_hbm, coarse_hbm, *rest,
    slots, sections, batch, hops
):
    parts = len(hops)
    outs = rest[:parts]
    (cur_buf, wh_ref, wl_ref, tw_ref, fine_ref, coarse_ref, turned_ref, mid_ref, acc_ref, in_sems) = rest[parts:]
    depths, _, rows, width = cur_ref.shape
    padded = 2 * width
    inner = padded // RADIX
    taps = width // RADIX
    tall = batch * rows
    groups = depths // batch
    me = lax.axis_index("lat")

    def load(g):
        return pltpu.make_async_copy(
            cur_ref.at[pl.ds(g * batch, batch)], cur_buf.at[pl.ds(g * batch, batch)], in_sems.at[g]
        )

    for g in range(groups):
        load(g).start()
    tables_in = copy_all([
        pltpu.make_async_copy(source, target, in_sems.at[groups + i])
        for i, (source, target) in enumerate([
            (wh_hbm, wh_ref), (wl_hbm, wl_ref), (tw_hbm, tw_ref), (fine_hbm, fine_ref), (coarse_hbm, coarse_ref)
        ])
    ])
    acc_ref[...] = jnp.zeros(acc_ref.shape, F32)

    @pl.loop(0, groups)
    def _(g):
        load(g).wait()
        for c in range(2):
            turned_ref[c] = cur_buf[pl.ds(g * batch, batch), c].reshape(tall, width).T
        pieces = []
        for r in range(RADIX):
            pieces.append(
                jnp.concatenate(
                    [turned_ref[c, pl.ds(r, taps, stride=RADIX), :].T for c in range(2)], axis=1
                )
            )

        @pl.when(g == 0)
        def _():
            wait_all(tables_in)

        mid_ref[...] = dot3(jnp.concatenate(pieces, axis=0), wh_ref[...], wl_ref[...])

        @pl.loop(0, batch)
        def _(jj):
            j = g * batch + jj
            turn = phase_rows(fine_ref, coarse_ref, off_ref[j])
            slot = plan_ref[1 + sections + j]
            for k in range(0, inner, LANES):
                values = []
                for r in range(RADIX):
                    at = pl.ds(r * tall + jj * rows, rows)
                    value = tuple(mid_ref[at, d * inner + k : d * inner + k + LANES] for d in range(2))
                    if r > 0:
                        value = cmul(value, tuple(tw_ref[d, r : r + 1, k : k + LANES] for d in range(2)))
                    values.append(value)
                for q, value in enumerate(butterfly(values, -1.0)):
                    lanes = slice(q * inner + k, q * inner + k + LANES)
                    b = (q * inner + k) // LANES
                    value = cmul(value, (turn[0][b : b + 1], turn[1][b : b + 1]))
                    for d in range(2):
                        acc_ref[slot, d, :, lanes] += value[d]

    half = LANES // 2
    side = lax.broadcasted_iota(jnp.int32, (rows, LANES), 1) // half

    @pl.loop(0, slots)
    def _(u):
        for out_ref, d in zip(outs, hops):
            peer = me ^ d
            odd = peer % 2
            lanes = pl.ds(pl.multiple_of(peer // 2 * LANES, LANES), LANES)
            still = acc_ref[u, odd, :, lanes]
            moved = pltpu.roll(acc_ref[u, 1 - odd, :, lanes], half, 1)
            out_ref[u] = jnp.where(side == odd, still, moved)


def couple_kernel(plan_ref, *rest, slots, hops):
    parts = len(hops)
    ins = rest[:parts]
    wh_ref, wl_ref, vh_ref, vl_ref, tw_ref, green_ref = rest[parts : parts + 6]
    outs = rest[parts + 6 : 2 * parts + 6]
    (order_buf, green_buf, spec_ref, mid_ref, lhs_ref, sems) = rest[2 * parts + 6 :]
    rows = ins[0].shape[1]
    columns, padded = green_buf.shape[3], green_buf.shape[4]
    inner = padded // RADIX
    taps = parts * rows // RADIX
    me = lax.axis_index("lat")

    def place(d):
        return pl.ds(pl.multiple_of((me ^ d) * rows, rows), rows)

    def fetch(t, s):
        return pltpu.make_async_copy(
            green_ref.at[plan_ref[1 + t], plan_ref[1 + s]], green_buf.at[t, s], sems.at[t, s]
        )

    @pl.loop(0, slots)
    def _(t):
        for s in range(slots):
            fetch(t, s).start()

    @pl.loop(0, slots)
    def _(u):
        for in_ref, d in zip(ins, hops):
            order_buf[place(d), :] = in_ref[u]
        blocks = []
        for r in range(RADIX):
            tall = order_buf[pl.ds(r, taps, stride=RADIX), :].T
            blocks.append(jnp.concatenate([tall[:columns], tall[columns:]], axis=1))
        mid_ref[...] = dot3(jnp.concatenate(blocks, axis=0), wh_ref[...], wl_ref[...])

        @pl.loop(0, columns // 16)
        def _(a16):
            for k in range(0, inner, LANES):
                values = []
                for r in range(RADIX):
                    at = pl.ds(pl.multiple_of(r * columns + a16 * 16, 16), 16)
                    value = tuple(mid_ref[at, d * inner + k : d * inner + k + LANES] for d in range(2))
                    if r > 0:
                        value = cmul(value, tuple(tw_ref[d, r : r + 1, k : k + LANES] for d in range(2)))
                    values.append(value)
                for q, value in enumerate(butterfly(values, -1.0)):
                    at = pl.ds(pl.multiple_of(a16 * 16, 16), 16)
                    for d in range(2):
                        spec_ref[u, d, at, q * inner + k : q * inner + k + LANES] = value[d]

    @pl.loop(0, slots)
    def _(t):
        for s in range(slots):
            fetch(t, s).wait()

        @pl.loop(0, columns // 8)
        def _(a8):
            at = pl.ds(pl.multiple_of(a8 * 8, 8), 8)
            for k in range(0, inner, LANES):
                coupled = []
                for q in range(RADIX):
                    lanes = slice(q * inner + k, q * inner + k + LANES)
                    total = None
                    for s in range(slots):
                        term = cmul(
                            tuple(green_buf[t, s, d, at, lanes] for d in range(2)),
                            tuple(spec_ref[s, d, at, lanes] for d in range(2)),
                        )
                        total = term if total is None else cadd(total, term)
                    coupled.append(total)
                for r, value in enumerate(butterfly(coupled, 1.0)):
                    if r > 0:
                        back = (tw_ref[0, r : r + 1, k : k + LANES], -tw_ref[1, r : r + 1, k : k + LANES])
                        value = cmul(value, back)
                    for d in range(2):
                        here = pl.ds(pl.multiple_of(r * columns + a8 * 8, 8), 8)
                        lhs_ref[here, d * inner + k : d * inner + k + LANES] = value[d]

        result = dot3(lhs_ref[...], vh_ref[...], vl_ref[...])
        for r in range(RADIX):
            block = result[r * columns : (r + 1) * columns]
            tall = jnp.concatenate([block[:, :taps], block[:, taps:]], axis=0).T
            order_buf[pl.ds(r, taps, stride=RADIX), :] = tall
        for out_ref, d in zip(outs, hops):
            out_ref[t] = order_buf[place(d), :]


def fields_kernel(plan_ref, off_ref, *rest, slots, sections, batch, hops):
    parts = len(hops)
    ins = rest[:parts]
    vh_ref, vl_ref, tw_ref, fine_ref, coarse_ref, out_hbm = rest[parts : parts + 6]
    out_ref, spec_ref, lhs_ref, turned_ref, out_sems = rest[parts + 6 :]
    depths, _, rows, width = out_ref.shape
    padded = 2 * width
    inner = padded // RADIX
    taps = width // RADIX
    tall = batch * rows
    groups = depths // batch
    half = LANES // 2
    low = lax.broadcasted_iota(jnp.int32, (rows, LANES), 1) < half
    me = lax.axis_index("lat")

    def store(g):
        at = pl.ds(g * batch, batch)
        return pltpu.make_async_copy(out_ref.at[at], out_hbm.at[at], out_sems.at[g])

    @pl.loop(0, slots)
    def _(u):
        for d in range(0, parts, 2):
            pair = ins[hops.index(d)][u], ins[hops.index(d + 1)][u]
            first = jnp.where(me % 2 == 0, pair[0], pair[1])
            second = jnp.where(me % 2 == 0, pair[1], pair[0])
            lanes = pl.ds(pl.multiple_of((me ^ d) // 2 * LANES, LANES), LANES)
            spec_ref[u, 0, :, lanes] = jnp.where(low, first, pltpu.roll(second, half, 1))
            spec_ref[u, 1, :, lanes] = jnp.where(low, pltpu.roll(first, half, 1), second)

    @pl.loop(0, groups)
    def _(g):
        @pl.loop(0, batch)
        def _(jj):
            j = g * batch + jj
            turn = phase_rows(fine_ref, coarse_ref, off_ref[j])
            slot = plan_ref[1 + sections + j]
            for k in range(0, inner, LANES):
                values = []
                for q in range(RADIX):
                    lanes = slice(q * inner + k, q * inner + k + LANES)
                    b = (q * inner + k) // LANES
                    value = tuple(spec_ref[slot, d, :, lanes] for d in range(2))
                    values.append(cmul(value, (turn[0][b : b + 1], -turn[1][b : b + 1])))
                for r, value in enumerate(butterfly(values, 1.0)):
                    if r > 0:
                        back = (tw_ref[0, r : r + 1, k : k + LANES], -tw_ref[1, r : r + 1, k : k + LANES])
                        value = cmul(value, back)
                    for d in range(2):
                        here = pl.ds(r * tall + jj * rows, rows)
                        lhs_ref[here, d * inner + k : d * inner + k + LANES] = value[d]

        result = dot3(lhs_ref[...], vh_ref[...], vl_ref[...])
        for d in range(2):
            for r in range(RADIX):
                block = result[r * tall : (r + 1) * tall, d * taps : (d + 1) * taps]
                turned_ref[d, pl.ds(r, taps, stride=RADIX), :] = block.T
            out_ref[pl.ds(g * batch, batch), d] = turned_ref[d].T.reshape(batch, rows, width)
        store(g).start()

    for g in range(groups):
        store(g).wait()


def vmem():
    return pl.BlockSpec(memory_space=pltpu.VMEM)


def anywhere():
    return pl.BlockSpec(memory_space=pl.ANY)


def smem():
    return pl.BlockSpec(memory_space=pltpu.SMEM)


def params(scratch, spare):
    held = sum(math.prod(a.shape) * jnp.dtype(a.dtype).itemsize for a in scratch)
    return pltpu.CompilerParams(vmem_limit_bytes=held + spare * 1024 * 1024)


def per_device(currents, green, section_map, offsets, *, parts):
    depths, _, rows, width = currents.shape
    sections = green.shape[0]
    columns = green.shape[3]
    padded = 2 * width
    inner = padded // RADIX
    taps = width // RADIX
    batch = LANES // rows
    hops = hop_order(parts)
    (wh, wl), (vh, vl), twiddle, fine, coarse = (
        jax.tree.map(jnp.asarray, entry) for entry in tables(width)
    )
    plan = pl.pallas_call(
        functools.partial(plan_kernel, depths=depths, sections=sections),
        out_shape=jax.ShapeDtypeStruct((1 + sections + depths,), jnp.int32),
        in_specs=[smem()],
        out_specs=smem(),
        name="plan",
    )(section_map)

    def exchange(sent):
        moved = [
            lax.ppermute(block, "lat", [(i, i ^ d) for i in range(parts)])
            for block, d in zip(sent[1:], hops[1:])
        ]
        return [sent[0], *moved]

    def run(slots, plan, offsets, currents, green, wh, wl, vh, vl, twiddle, fine, coarse):
        groups = depths // batch
        blocks = [jax.ShapeDtypeStruct((slots, rows, LANES), F32)] * parts
        dma = pltpu.SemaphoreType.DMA
        room = [
            pltpu.VMEM(currents.shape, F32),
            pltpu.VMEM(wh.shape, BF16),
            pltpu.VMEM(wl.shape, BF16),
            pltpu.VMEM(twiddle.shape, F32),
            pltpu.VMEM(fine.shape, F32),
            pltpu.VMEM(coarse.shape, F32),
            pltpu.VMEM((2, width, LANES), F32),
            pltpu.VMEM((RADIX * LANES, 2 * inner), F32),
            pltpu.VMEM((slots, 2, rows, padded), F32),
        ]
        sent = pl.pallas_call(
            functools.partial(rows_kernel, slots=slots, sections=sections, batch=batch, hops=hops),
            out_shape=blocks,
            in_specs=[smem(), smem()] + [anywhere()] * 6,
            out_specs=[vmem()] * parts,
            scratch_shapes=room + [dma((groups + 5,))],
            compiler_params=params(room, 10),
            name=f"rows_{slots}",
        )(plan, offsets, currents, wh, wl, twiddle, fine, coarse)
        got = exchange(sent)
        room = [
            pltpu.VMEM((width, LANES), F32),
            pltpu.VMEM((slots, slots, 2, columns, padded), F32),
            pltpu.VMEM((slots, 2, columns, padded), F32),
            pltpu.VMEM((RADIX * columns, 2 * inner), F32),
            pltpu.VMEM((RADIX * columns, 2 * inner), F32),
        ]
        back = pl.pallas_call(
            functools.partial(couple_kernel, slots=slots, hops=hops),
            out_shape=blocks,
            in_specs=[smem()] + [vmem()] * (parts + 5) + [anywhere()],
            out_specs=[vmem()] * parts,
            scratch_shapes=room + [dma((slots, slots))],
            compiler_params=params(room, 10),
            name=f"couple_{slots}",
        )(plan, *got, wh, wl, vh, vl, twiddle, green)
        home = exchange(back)
        room = [
            pltpu.VMEM(currents.shape, F32),
            pltpu.VMEM((slots, 2, rows, padded), F32),
            pltpu.VMEM((RADIX * LANES, 2 * inner), F32),
            pltpu.VMEM((2, width, LANES), F32),
        ]
        return pl.pallas_call(
            functools.partial(fields_kernel, slots=slots, sections=sections, batch=batch, hops=hops),
            out_shape=jax.ShapeDtypeStruct(currents.shape, F32),
            in_specs=[smem(), smem()] + [vmem()] * (parts + 5),
            out_specs=anywhere(),
            scratch_shapes=room + [dma((groups,))],
            compiler_params=params(room, 10),
            name=f"fields_{slots}",
        )(plan, offsets, *home, vh, vl, twiddle, fine, coarse)

    least = max(1, (min(depths, sections) + 1) // 2 + 1)
    choices = list(range(least, min(depths, sections) + 1))
    return lax.switch(
        jnp.maximum(plan[0] - least, 0),
        [functools.partial(run, slots) for slots in choices],
        plan, offsets, currents, green, wh, wl, vh, vl, twiddle, fine, coarse,
    )


def solution(mesh):
    parts = mesh.shape["lat"]

    def body(currents, green, section_map, offsets):
        depths, _, rows, width = currents.shape
        columns = green.shape[3]
        fits = (
            2 * columns == LANES
            and rows % (8 * RADIX) == 0
            and LANES % rows == 0
            and depths % (LANES // rows) == 0
            and width % (RADIX * LANES) == 0
            and columns * parts == 2 * width
            and parts & (parts - 1) == 0
        )
        if fits:
            return per_device(currents, green, section_map, offsets, parts=parts)
        return plain_per_device(currents, green, section_map, offsets)

    in_specs = (
        P("group", None, "lat", None),
        P("group", None, None, "lat", None),
        P("group"),
        P("group"),
    )
    out_specs = P("group", None, "lat", None)
    return jax.shard_map(
        body, mesh=mesh, in_specs=in_specs, out_specs=out_specs, check_vma=False
    )
```

```python
import functools
import math

import jax
import jax.numpy as jnp
import numpy as np
from jax import lax
from jax.experimental import pallas as pl
from jax.experimental.pallas import tpu as pltpu
from jax.sharding import PartitionSpec as P

RADIX = 4
LANES = 128
FINE = 32
F32 = jnp.float32
BF16 = jnp.bfloat16


def dft_table(n_in, n_out, period, sign_value):
    row_ids = lax.iota(jnp.int32, n_in)
    col_ids = lax.iota(jnp.int32, n_out)
    angles = (
        2.0 * math.pi / period * (row_ids[:, None] * col_ids[None, :] % period).astype(jnp.float32)
    )
    cosine = jnp.cos(angles)
    sine_part = sign_value * jnp.sin(angles)
    return jnp.stack(
        [jnp.stack([cosine, sine_part], axis=1), jnp.stack([-sine_part, cosine], axis=1)], axis=0
    )


def phases(offsets, period, sign_value):
    col_ids = lax.iota(jnp.int32, period)
    angles = (
        2.0 * math.pi / period * (offsets[:, None] * col_ids[None, :] % period).astype(jnp.float32)
    )
    return (jnp.cos(angles)[:, None, :], sign_value * jnp.sin(angles)[:, None, :])


def rotate(planes, cosine, sine_part):
    real_part = planes[:, 0] * cosine - planes[:, 1] * sine_part
    imag_part = planes[:, 0] * sine_part + planes[:, 1] * cosine
    return jnp.stack([real_part, imag_part], axis=1)


def plain_per_device(currents, green, section_map, offsets):
    highest = lax.Precision.HIGHEST
    plane_width = currents.shape[3]
    padded = 2 * plane_width
    sections = green.shape[0]
    forward = dft_table(plane_width, padded, padded, -1.0)
    inverse = dft_table(padded, plane_width, padded, 1.0)
    onehot = (section_map[:, None] == lax.iota(jnp.int32, sections)[None, :]).astype(jnp.float32)
    spec_y = jnp.einsum("jcxy,cydk->jdxk", currents, forward, precision=highest)
    cos_fwd, sin_fwd = phases(offsets, padded, -1.0)
    shifted = jnp.transpose(rotate(spec_y, cos_fwd, sin_fwd), (0, 2, 1, 3))
    grouped = jnp.einsum("js,jxdk->sxdk", onehot, shifted, precision=highest)
    spectra = jnp.einsum(
        "mxcq,cxdk->mdqk",
        lax.all_to_all(grouped, "lat", split_axis=3, concat_axis=1, tiled=True),
        forward,
        precision=highest,
    )
    green_real = green[:, :, 0]
    green_imag = green[:, :, 1]
    out_real = jnp.einsum(
        "tsqk,sqk->tqk", green_real, spectra[:, 0], precision=highest
    ) - jnp.einsum("tsqk,sqk->tqk", green_imag, spectra[:, 1], precision=highest)
    out_imag = jnp.einsum(
        "tsqk,sqk->tqk", green_real, spectra[:, 1], precision=highest
    ) + jnp.einsum("tsqk,sqk->tqk", green_imag, spectra[:, 0], precision=highest)
    coupled = jnp.stack([out_real, out_imag], axis=1)
    returned = lax.all_to_all(
        jnp.einsum("mcqk,ckdx->mdxq", coupled, inverse, precision=highest),
        "lat",
        split_axis=2,
        concat_axis=3,
        tiled=True,
    )
    per_depth = jnp.einsum("js,sdxq->jdxq", onehot, returned, precision=highest)
    cos_back, sin_back = phases(offsets, padded, 1.0)
    turned = rotate(per_depth, cos_back, sin_back)
    result = jnp.einsum("jcxk,ckdy->jdxy", turned, inverse, precision=highest)
    return result * (1.0 / (padded * padded))


def split_np(table):
    high = table.astype(BF16)
    low = (table - high.astype(np.float64)).astype(BF16)
    return high, low


def unit(products, period):
    angles = (2.0 * math.pi / period) * (products % period).astype(np.float64)
    return np.cos(angles), np.sin(angles)


def tables(width):
    padded = 2 * width
    inner = padded // RADIX
    taps = width // RADIX
    cosine, sine = unit(np.arange(taps)[:, None] * np.arange(inner)[None, :], inner)
    weights = np.concatenate(
        [np.concatenate([cosine, -sine], axis=1), np.concatenate([sine, cosine], axis=1)], axis=0
    )
    forward = split_np(weights)
    inverse = split_np(np.ascontiguousarray(weights.T) / (padded * 1.0))
    cosine, sine = unit(np.arange(8)[:, None] * np.arange(inner)[None, :], padded)
    twiddle = np.stack([cosine, -sine]).astype(np.float32)
    lanes = np.arange(padded).reshape(1, padded // LANES, LANES)
    cosine, sine = unit(np.arange(FINE)[:, None, None] * lanes, padded)
    fine = np.stack([cosine, -sine]).astype(np.float32)
    cosine, sine = unit(FINE * np.arange(width // FINE + 1)[:, None, None] * lanes[:, :1], padded)
    coarse = np.stack([cosine, -sine]).astype(np.float32)
    return forward, inverse, twiddle, fine, coarse


def cmul(a, b):
    return a[0] * b[0] - a[1] * b[1], a[0] * b[1] + a[1] * b[0]


def cadd(a, b):
    return a[0] + b[0], a[1] + b[1]


def csub(a, b):
    return a[0] - b[0], a[1] - b[1]


def butterfly(v, turn):
    even, odd = cadd(v[0], v[2]), csub(v[0], v[2])
    cross, diff = cadd(v[1], v[3]), csub(v[1], v[3])
    spun = (-turn * diff[1], turn * diff[0])
    return cadd(even, cross), cadd(odd, spun), csub(even, cross), csub(odd, spun)


def split(value):
    high = value.astype(BF16)
    return high, (value - high.astype(F32)).astype(BF16)


def dot3(value, high_table, low_table):
    high, low = split(value)
    dot = functools.partial(jnp.dot, preferred_element_type=F32)
    return dot(high, high_table) + (dot(high, low_table) + dot(low, high_table))


def phase_rows(fine_ref, coarse_ref, offset):
    fine_id = offset % FINE
    coarse_id = offset // FINE
    return cmul(
        tuple(fine_ref[d, fine_id] for d in range(2)),
        tuple(coarse_ref[d, coarse_id] for d in range(2)),
    )


def make_plan(map_ref, plan_ref, *, depths, sections):
    count = jnp.int32(0)
    for u in range(sections):
        plan_ref[1 + u] = jnp.int32(0)
    ids = [map_ref[j] for j in range(depths)]
    for s in range(sections):
        used = jnp.int32(0)
        for j in range(depths):
            used = jnp.maximum(used, (ids[j] == s).astype(jnp.int32))

        @pl.when(used > 0)
        def _(s=s, count=count):
            plan_ref[1 + count] = jnp.int32(s)
            for j in range(depths):
                @pl.when(ids[j] == s)
                def _(j=j):
                    plan_ref[1 + sections + j] = count

        count = count + used
    plan_ref[0] = count


def hop_order(parts):
    quarter = max(parts // 4, 1)
    far = [d for low in range(quarter) for d in (2 * quarter + low, 3 * quarter + low) if d < parts]
    near = [d for d in range(quarter, 2 * quarter)] + [d for d in range(quarter - 1, 0, -1)]
    return (0, *far[:4], *near[:1], *far[4:], *near[1:])


def copy_all(copies):
    for copy in copies:
        copy.start()
    return copies


def wait_all(copies):
    for copy in copies:
        copy.wait()


def rows_kernel(
    map_hbm, off_hbm, cur_ref, wh_hbm, wl_hbm, tw_hbm, fine_hbm, coarse_hbm, plan_ref, acc_ref,
    cur_buf, wh_ref, wl_ref, tw_ref, fine_ref, coarse_ref, turned_ref, mid_ref, map_ref, off_ref, in_sems,
    *, sections, batch
):
    depths, _, rows, width = cur_ref.shape
    padded = 2 * width
    inner = padded // RADIX
    taps = width // RADIX
    tall = batch * rows
    groups = depths // batch

    def load(g):
        return pltpu.make_async_copy(
            cur_ref.at[pl.ds(g * batch, batch)], cur_buf.at[pl.ds(g * batch, batch)], in_sems.at[g]
        )

    for g in range(groups):
        load(g).start()
    tables_in = copy_all([
        pltpu.make_async_copy(source, target, in_sems.at[groups + i])
        for i, (source, target) in enumerate([
            (wh_hbm, wh_ref), (wl_hbm, wl_ref), (tw_hbm, tw_ref), (fine_hbm, fine_ref), (coarse_hbm, coarse_ref)
        ])
    ])
    scalars_in = copy_all([
        pltpu.make_async_copy(map_hbm, map_ref, in_sems.at[groups + 5]),
        pltpu.make_async_copy(off_hbm, off_ref, in_sems.at[groups + 6]),
    ])
    acc_ref[...] = jnp.zeros(acc_ref.shape, F32)
    wait_all(scalars_in)
    make_plan(map_ref, plan_ref, depths=depths, sections=sections)

    @pl.loop(0, groups)
    def _(g):
        load(g).wait()
        for c in range(2):
            turned_ref[c] = cur_buf[pl.ds(g * batch, batch), c].reshape(tall, width).T
        pieces = []
        for r in range(RADIX):
            pieces.append(
                jnp.concatenate(
                    [turned_ref[c, pl.ds(r, taps, stride=RADIX), :].T for c in range(2)], axis=1
                )
            )

        @pl.when(g == 0)
        def _():
            wait_all(tables_in)

        mid_ref[...] = dot3(jnp.concatenate(pieces, axis=0), wh_ref[...], wl_ref[...])

        @pl.loop(0, batch)
        def _(jj):
            j = g * batch + jj
            turn = phase_rows(fine_ref, coarse_ref, off_ref[j])
            slot = plan_ref[1 + sections + j]
            for k in range(0, inner, LANES):
                values = []
                for r in range(RADIX):
                    at = pl.ds(r * tall + jj * rows, rows)
                    value = tuple(mid_ref[at, d * inner + k : d * inner + k + LANES] for d in range(2))
                    if r > 0:
                        value = cmul(value, tuple(tw_ref[d, r : r + 1, k : k + LANES] for d in range(2)))
                    values.append(value)
                for q, value in enumerate(butterfly(values, -1.0)):
                    lanes = slice(q * inner + k, q * inner + k + LANES)
                    b = (q * inner + k) // LANES
                    value = cmul(value, (turn[0][b : b + 1], turn[1][b : b + 1]))
                    for d in range(2):
                        acc_ref[slot, d, :, lanes] += value[d]


def pack_kernel(acc_ref, *rest, slots, hops):
    parts = len(hops)
    outs = rest[:parts]
    stage_ref = rest[parts]
    _, _, rows, padded = acc_ref.shape
    me = lax.axis_index("lat")
    half = LANES // 2
    low = lax.broadcasted_iota(jnp.int32, (rows, LANES), 1) < half

    @pl.loop(0, slots)
    def _(u):
        for b in range(padded // LANES):
            lanes = slice(b * LANES, (b + 1) * LANES)
            re = acc_ref[u, 0, :, lanes]
            im = acc_ref[u, 1, :, lanes]
            stage_ref[2 * b] = jnp.where(low, re, pltpu.roll(im, half, 1))
            stage_ref[2 * b + 1] = jnp.where(low, pltpu.roll(re, half, 1), im)
        for out_ref, d in zip(outs, hops):
            out_ref[u] = stage_ref[me ^ d]


def couple_kernel(plan_ref, *rest, slots, hops):
    parts = len(hops)
    ins = rest[:parts]
    wh_ref, wl_ref, vh_ref, vl_ref, tw_ref, green_ref = rest[parts : parts + 6]
    outs = rest[parts + 6 : 2 * parts + 6]
    (order_buf, green_buf, spec_ref, mid_ref, lhs_ref, sems) = rest[2 * parts + 6 :]
    rows = ins[0].shape[1]
    columns, padded = green_buf.shape[3], green_buf.shape[4]
    inner = padded // RADIX
    taps = parts * rows // RADIX
    me = lax.axis_index("lat")

    def place(d):
        return pl.ds(pl.multiple_of((me ^ d) * rows, rows), rows)

    def fetch(t, s):
        return pltpu.make_async_copy(
            green_ref.at[plan_ref[1 + t], plan_ref[1 + s]], green_buf.at[t, s], sems.at[t, s]
        )

    @pl.loop(0, slots)
    def _(t):
        for s in range(slots):
            fetch(t, s).start()

    def transform(first, count):
        blocks = []
        for i in range(count):
            for in_ref, d in zip(ins, hops):
                order_buf[i, place(d), :] = in_ref[first + i]
            for r in range(RADIX):
                tall = order_buf[i, pl.ds(r, taps, stride=RADIX), :].T
                blocks.append(jnp.concatenate([tall[:columns], tall[columns:]], axis=1))
        mid_ref[: count * RADIX * columns] = dot3(jnp.concatenate(blocks, axis=0), wh_ref[...], wl_ref[...])

        @pl.loop(0, columns // 16)
        def _(a16):
            for i in range(count):
                for k in range(0, inner, LANES):
                    values = []
                    for r in range(RADIX):
                        at = pl.ds(pl.multiple_of((i * RADIX + r) * columns + a16 * 16, 16), 16)
                        value = tuple(mid_ref[at, d * inner + k : d * inner + k + LANES] for d in range(2))
                        if r > 0:
                            value = cmul(value, tuple(tw_ref[d, r : r + 1, k : k + LANES] for d in range(2)))
                        values.append(value)
                    for q, value in enumerate(butterfly(values, -1.0)):
                        at = pl.ds(pl.multiple_of(a16 * 16, 16), 16)
                        for d in range(2):
                            spec_ref[first + i, d, at, q * inner + k : q * inner + k + LANES] = value[d]

    @pl.loop(0, slots // 2)
    def _(pair):
        transform(2 * pair, 2)

    if slots % 2:
        transform(slots - 1, 1)

    def receive(first, count):
        for i in range(count):
            for s in range(slots):
                fetch(first + i, s).wait()

        @pl.loop(0, columns // 8)
        def _(a8):
            at = pl.ds(pl.multiple_of(a8 * 8, 8), 8)
            for k in range(0, inner, LANES):
                coupled = [[] for _ in range(count)]
                for q in range(RADIX):
                    lanes = slice(q * inner + k, q * inner + k + LANES)
                    totals = [None] * count
                    for s in range(slots):
                        source = tuple(spec_ref[s, d, at, lanes] for d in range(2))
                        for i in range(count):
                            factor = tuple(green_buf[first + i, s, d, at, lanes] for d in range(2))
                            term = cmul(factor, source)
                            totals[i] = term if totals[i] is None else cadd(totals[i], term)
                    for i in range(count):
                        coupled[i].append(totals[i])
                for i in range(count):
                    for r, value in enumerate(butterfly(coupled[i], 1.0)):
                        if r > 0:
                            back = (tw_ref[0, r : r + 1, k : k + LANES], -tw_ref[1, r : r + 1, k : k + LANES])
                            value = cmul(value, back)
                        for d in range(2):
                            here = pl.ds(pl.multiple_of((i * RADIX + r) * columns + a8 * 8, 8), 8)
                            lhs_ref[here, d * inner + k : d * inner + k + LANES] = value[d]

        result = dot3(lhs_ref[: count * RADIX * columns], vh_ref[...], vl_ref[...])
        for i in range(count):
            for r in range(RADIX):
                block = result[(i * RADIX + r) * columns : (i * RADIX + r + 1) * columns]
                tall = jnp.concatenate([block[:, :taps], block[:, taps:]], axis=0).T
                order_buf[i, pl.ds(r, taps, stride=RADIX), :] = tall
            for out_ref, d in zip(outs, hops):
                out_ref[first + i] = order_buf[i, place(d), :]

    @pl.loop(0, slots // 2)
    def _(pair):
        receive(2 * pair, 2)

    if slots % 2:
        receive(slots - 1, 1)


def fields_kernel(plan_ref, off_ref, *rest, slots, sections, batch, hops):
    parts = len(hops)
    ins = rest[:parts]
    vh_ref, vl_ref, tw_ref, fine_ref, coarse_ref, out_hbm = rest[parts : parts + 6]
    out_ref, spec_ref, lhs_ref, turned_ref, stage_ref, out_sems = rest[parts + 6 :]
    depths, _, rows, width = out_ref.shape
    padded = 2 * width
    inner = padded // RADIX
    taps = width // RADIX
    tall = batch * rows
    groups = depths // batch
    half = LANES // 2
    low = lax.broadcasted_iota(jnp.int32, (rows, LANES), 1) < half
    me = lax.axis_index("lat")

    def store(g):
        at = pl.ds(g * batch, batch)
        return pltpu.make_async_copy(out_ref.at[at], out_hbm.at[at], out_sems.at[g])

    @pl.loop(0, slots)
    def _(u):
        for in_ref, d in zip(ins, hops):
            stage_ref[me ^ d] = in_ref[u]
        for b in range(padded // LANES):
            lanes = slice(b * LANES, (b + 1) * LANES)
            first = stage_ref[2 * b]
            second = stage_ref[2 * b + 1]
            spec_ref[u, 0, :, lanes] = jnp.where(low, first, pltpu.roll(second, half, 1))
            spec_ref[u, 1, :, lanes] = jnp.where(low, pltpu.roll(first, half, 1), second)

    @pl.loop(0, groups)
    def _(g):
        @pl.loop(0, batch)
        def _(jj):
            j = g * batch + jj
            turn = phase_rows(fine_ref, coarse_ref, off_ref[j])
            slot = plan_ref[1 + sections + j]
            for k in range(0, inner, LANES):
                values = []
                for q in range(RADIX):
                    lanes = slice(q * inner + k, q * inner + k + LANES)
                    b = (q * inner + k) // LANES
                    value = tuple(spec_ref[slot, d, :, lanes] for d in range(2))
                    values.append(cmul(value, (turn[0][b : b + 1], -turn[1][b : b + 1])))
                for r, value in enumerate(butterfly(values, 1.0)):
                    if r > 0:
                        back = (tw_ref[0, r : r + 1, k : k + LANES], -tw_ref[1, r : r + 1, k : k + LANES])
                        value = cmul(value, back)
                    for d in range(2):
                        here = pl.ds(r * tall + jj * rows, rows)
                        lhs_ref[here, d * inner + k : d * inner + k + LANES] = value[d]

        result = dot3(lhs_ref[...], vh_ref[...], vl_ref[...])
        for d in range(2):
            for r in range(RADIX):
                block = result[r * tall : (r + 1) * tall, d * taps : (d + 1) * taps]
                turned_ref[d, pl.ds(r, taps, stride=RADIX), :] = block.T
            out_ref[pl.ds(g * batch, batch), d] = turned_ref[d].T.reshape(batch, rows, width)
        store(g).start()

    for g in range(groups):
        store(g).wait()


def vmem():
    return pl.BlockSpec(memory_space=pltpu.VMEM)


def anywhere():
    return pl.BlockSpec(memory_space=pl.ANY)


def smem():
    return pl.BlockSpec(memory_space=pltpu.SMEM)


def params(scratch, spare):
    held = sum(math.prod(a.shape) * jnp.dtype(a.dtype).itemsize for a in scratch)
    return pltpu.CompilerParams(vmem_limit_bytes=held + spare * 1024 * 1024)


def per_device(currents, green, section_map, offsets, *, parts):
    depths, _, rows, width = currents.shape
    sections = green.shape[0]
    columns = green.shape[3]
    padded = 2 * width
    inner = padded // RADIX
    taps = width // RADIX
    batch = LANES // rows
    hops = hop_order(parts)
    (wh, wl), (vh, vl), twiddle, fine, coarse = (
        jax.tree.map(jnp.asarray, entry) for entry in tables(width)
    )
    groups = depths // batch
    dma = pltpu.SemaphoreType.DMA
    most = min(depths, sections)
    room = [
        pltpu.VMEM(currents.shape, F32),
        pltpu.VMEM(wh.shape, BF16),
        pltpu.VMEM(wl.shape, BF16),
        pltpu.VMEM(twiddle.shape, F32),
        pltpu.VMEM(fine.shape, F32),
        pltpu.VMEM(coarse.shape, F32),
        pltpu.VMEM((2, width, LANES), F32),
        pltpu.VMEM((RADIX * LANES, 2 * inner), F32),
    ]
    in_hbm = functools.partial(pltpu.with_memory_space_constraint, memory_space=pltpu.HBM)
    plan, acc = pl.pallas_call(
        functools.partial(rows_kernel, sections=sections, batch=batch),
        out_shape=[
            jax.ShapeDtypeStruct((1 + sections + depths,), jnp.int32),
            pltpu.VMEM((most, 2, rows, padded), F32),
        ],
        in_specs=[anywhere()] * 8,
        out_specs=[smem(), vmem()],
        scratch_shapes=room + [
            pltpu.SMEM(section_map.shape, jnp.int32),
            pltpu.SMEM(offsets.shape, jnp.int32),
            dma((groups + 7,)),
        ],
        compiler_params=params(room, 10),
        name="rows",
    )(in_hbm(section_map), in_hbm(offsets), in_hbm(currents), wh, wl, twiddle, fine, coarse)

    def exchange(sent):
        moved = [
            lax.ppermute(block, "lat", [(i, i ^ d) for i in range(parts)])
            for block, d in zip(sent[1:], hops[1:])
        ]
        return [sent[0], *moved]

    def run(slots, plan, acc, offsets, green, wh, wl, vh, vl, twiddle, fine, coarse):
        blocks = [jax.ShapeDtypeStruct((slots, rows, LANES), F32)] * parts
        room = [pltpu.VMEM((parts, rows, LANES), F32)]
        sent = pl.pallas_call(
            functools.partial(pack_kernel, slots=slots, hops=hops),
            out_shape=blocks,
            in_specs=[vmem()],
            out_specs=[vmem()] * parts,
            scratch_shapes=room,
            compiler_params=params(room, 4),
            name=f"pack_{slots}",
        )(acc)
        got = exchange(sent)
        room = [
            pltpu.VMEM((2, width, LANES), F32),
            pltpu.VMEM((slots, slots, 2, columns, padded), F32),
            pltpu.VMEM((slots, 2, columns, padded), F32),
            pltpu.VMEM((2 * RADIX * columns, 2 * inner), F32),
            pltpu.VMEM((2 * RADIX * columns, 2 * inner), F32),
        ]
        back = pl.pallas_call(
            functools.partial(couple_kernel, slots=slots, hops=hops),
            out_shape=blocks,
            in_specs=[smem()] + [vmem()] * (parts + 5) + [anywhere()],
            out_specs=[vmem()] * parts,
            scratch_shapes=room + [dma((slots, slots))],
            compiler_params=params(room, 10),
            name=f"couple_{slots}",
        )(plan, *got, wh, wl, vh, vl, twiddle, green)
        home = exchange(back)
        room = [
            pltpu.VMEM(currents.shape, F32),
            pltpu.VMEM((slots, 2, rows, padded), F32),
            pltpu.VMEM((RADIX * LANES, 2 * inner), F32),
            pltpu.VMEM((2, width, LANES), F32),
            pltpu.VMEM((parts, rows, LANES), F32),
        ]
        return pl.pallas_call(
            functools.partial(fields_kernel, slots=slots, sections=sections, batch=batch, hops=hops),
            out_shape=pltpu.HBM(currents.shape, F32),
            in_specs=[smem(), smem()] + [vmem()] * (parts + 5),
            out_specs=anywhere(),
            scratch_shapes=room + [dma((groups,))],
            compiler_params=params(room, 10),
            name=f"fields_{slots}",
        )(plan, offsets, *home, vh, vl, twiddle, fine, coarse)

    least = max(1, (most + 1) // 2 + 1)
    choices = list(range(least, most + 1))
    return lax.switch(
        jnp.maximum(plan[0] - least, 0),
        [functools.partial(run, slots) for slots in choices],
        plan, acc, offsets, green, wh, wl, vh, vl, twiddle, fine, coarse,
    )


def solution(mesh):
    parts = mesh.shape["lat"]

    def body(currents, green, section_map, offsets):
        depths, _, rows, width = currents.shape
        columns = green.shape[3]
        fits = (
            2 * columns == LANES
            and rows % (8 * RADIX) == 0
            and LANES % rows == 0
            and depths % (LANES // rows) == 0
            and width % (RADIX * LANES) == 0
            and columns * parts == 2 * width
            and parts & (parts - 1) == 0
        )
        if fits:
            return per_device(currents, green, section_map, offsets, parts=parts)
        return plain_per_device(currents, green, section_map, offsets)

    in_specs = (
        P("group", None, "lat", None),
        P("group", None, None, "lat", None),
        P("group"),
        P("group"),
    )
    out_specs = P("group", None, "lat", None)
    return jax.shard_map(
        body, mesh=mesh, in_specs=in_specs, out_specs=out_specs, check_vma=False
    )
```

```python
import functools
import math

import jax
import jax.numpy as jnp
import numpy as np
from jax import lax
from jax.experimental import pallas as pl
from jax.experimental.pallas import tpu as pltpu
from jax.sharding import PartitionSpec as P

RADIX = 4
LANES = 128
FINE = 32
F32 = jnp.float32
BF16 = jnp.bfloat16


def dft_table(n_in, n_out, period, sign_value):
    row_ids = lax.iota(jnp.int32, n_in)
    col_ids = lax.iota(jnp.int32, n_out)
    angles = (
        2.0 * math.pi / period * (row_ids[:, None] * col_ids[None, :] % period).astype(jnp.float32)
    )
    cosine = jnp.cos(angles)
    sine_part = sign_value * jnp.sin(angles)
    return jnp.stack(
        [jnp.stack([cosine, sine_part], axis=1), jnp.stack([-sine_part, cosine], axis=1)], axis=0
    )


def phases(offsets, period, sign_value):
    col_ids = lax.iota(jnp.int32, period)
    angles = (
        2.0 * math.pi / period * (offsets[:, None] * col_ids[None, :] % period).astype(jnp.float32)
    )
    return (jnp.cos(angles)[:, None, :], sign_value * jnp.sin(angles)[:, None, :])


def rotate(planes, cosine, sine_part):
    real_part = planes[:, 0] * cosine - planes[:, 1] * sine_part
    imag_part = planes[:, 0] * sine_part + planes[:, 1] * cosine
    return jnp.stack([real_part, imag_part], axis=1)


def plain_per_device(currents, green, section_map, offsets):
    highest = lax.Precision.HIGHEST
    plane_width = currents.shape[3]
    padded = 2 * plane_width
    sections = green.shape[0]
    forward = dft_table(plane_width, padded, padded, -1.0)
    inverse = dft_table(padded, plane_width, padded, 1.0)
    onehot = (section_map[:, None] == lax.iota(jnp.int32, sections)[None, :]).astype(jnp.float32)
    spec_y = jnp.einsum("jcxy,cydk->jdxk", currents, forward, precision=highest)
    cos_fwd, sin_fwd = phases(offsets, padded, -1.0)
    shifted = jnp.transpose(rotate(spec_y, cos_fwd, sin_fwd), (0, 2, 1, 3))
    grouped = jnp.einsum("js,jxdk->sxdk", onehot, shifted, precision=highest)
    spectra = jnp.einsum(
        "mxcq,cxdk->mdqk",
        lax.all_to_all(grouped, "lat", split_axis=3, concat_axis=1, tiled=True),
        forward,
        precision=highest,
    )
    green_real = green[:, :, 0]
    green_imag = green[:, :, 1]
    out_real = jnp.einsum(
        "tsqk,sqk->tqk", green_real, spectra[:, 0], precision=highest
    ) - jnp.einsum("tsqk,sqk->tqk", green_imag, spectra[:, 1], precision=highest)
    out_imag = jnp.einsum(
        "tsqk,sqk->tqk", green_real, spectra[:, 1], precision=highest
    ) + jnp.einsum("tsqk,sqk->tqk", green_imag, spectra[:, 0], precision=highest)
    coupled = jnp.stack([out_real, out_imag], axis=1)
    returned = lax.all_to_all(
        jnp.einsum("mcqk,ckdx->mdxq", coupled, inverse, precision=highest),
        "lat",
        split_axis=2,
        concat_axis=3,
        tiled=True,
    )
    per_depth = jnp.einsum("js,sdxq->jdxq", onehot, returned, precision=highest)
    cos_back, sin_back = phases(offsets, padded, 1.0)
    turned = rotate(per_depth, cos_back, sin_back)
    result = jnp.einsum("jcxk,ckdy->jdxy", turned, inverse, precision=highest)
    return result * (1.0 / (padded * padded))


def split_np(table):
    high = table.astype(BF16)
    low = (table - high.astype(np.float64)).astype(BF16)
    return high, low


def unit(products, period):
    angles = (2.0 * math.pi / period) * (products % period).astype(np.float64)
    return np.cos(angles), np.sin(angles)


def tables(width):
    padded = 2 * width
    inner = padded // RADIX
    taps = width // RADIX
    cosine, sine = unit(np.arange(taps)[:, None] * np.arange(inner)[None, :], inner)
    weights = np.concatenate(
        [np.concatenate([cosine, -sine], axis=1), np.concatenate([sine, cosine], axis=1)], axis=0
    )
    forward = split_np(weights)
    inverse = split_np(np.ascontiguousarray(weights.T) / (padded * 1.0))
    cosine, sine = unit(np.arange(8)[:, None] * np.arange(inner)[None, :], padded)
    twiddle = np.stack([cosine, -sine]).astype(np.float32)
    lanes = np.arange(padded).reshape(1, padded // LANES, LANES)
    cosine, sine = unit(np.arange(FINE)[:, None, None] * lanes, padded)
    fine = np.stack([cosine, -sine]).astype(np.float32)
    cosine, sine = unit(FINE * np.arange(width // FINE + 1)[:, None, None] * lanes[:, :1], padded)
    coarse = np.stack([cosine, -sine]).astype(np.float32)
    return forward, inverse, twiddle, fine, coarse


def cmul(a, b):
    return a[0] * b[0] - a[1] * b[1], a[0] * b[1] + a[1] * b[0]


def cadd(a, b):
    return a[0] + b[0], a[1] + b[1]


def csub(a, b):
    return a[0] - b[0], a[1] - b[1]


def butterfly(v, turn):
    even, odd = cadd(v[0], v[2]), csub(v[0], v[2])
    cross, diff = cadd(v[1], v[3]), csub(v[1], v[3])
    spun = (-turn * diff[1], turn * diff[0])
    return cadd(even, cross), cadd(odd, spun), csub(even, cross), csub(odd, spun)


def split(value):
    high = value.astype(BF16)
    return high, (value - high.astype(F32)).astype(BF16)


def dot3(value, high_table, low_table):
    high, low = split(value)
    dot = functools.partial(jnp.dot, preferred_element_type=F32)
    return dot(high, high_table) + (dot(high, low_table) + dot(low, high_table))


def phase_rows(fine_ref, coarse_ref, offset):
    fine_id = offset % FINE
    coarse_id = offset // FINE
    return cmul(
        tuple(fine_ref[d, fine_id] for d in range(2)),
        tuple(coarse_ref[d, coarse_id] for d in range(2)),
    )


def make_plan(map_ref, plan_ref, *, depths, sections):
    count = jnp.int32(0)
    for u in range(sections):
        plan_ref[1 + u] = jnp.int32(0)
    ids = [map_ref[j] for j in range(depths)]
    for s in range(sections):
        used = jnp.int32(0)
        for j in range(depths):
            used = jnp.maximum(used, (ids[j] == s).astype(jnp.int32))

        @pl.when(used > 0)
        def _(s=s, count=count):
            plan_ref[1 + count] = jnp.int32(s)
            for j in range(depths):
                @pl.when(ids[j] == s)
                def _(j=j):
                    plan_ref[1 + sections + j] = count

        count = count + used
    plan_ref[0] = count


def trade_halves(x, y, low):
    kept = jnp.where(low, x, y)
    moved = pltpu.roll(jnp.where(low, y, x), LANES // 2, 1)
    return jnp.where(low, kept, moved), jnp.where(low, moved, kept)


def hop_order(parts):
    quarter = max(parts // 4, 1)
    far = [d for low in range(quarter) for d in (2 * quarter + low, 3 * quarter + low) if d < parts]
    near = [d for d in range(quarter, 2 * quarter)] + [d for d in range(quarter - 1, 0, -1)]
    return (0, *far[:4], *near[:1], *far[4:], *near[1:])


def copy_all(copies):
    for copy in copies:
        copy.start()
    return copies


def wait_all(copies):
    for copy in copies:
        copy.wait()


def rows_kernel(
    map_hbm, off_hbm, cur_ref, wh_hbm, wl_hbm, tw_hbm, fine_hbm, coarse_hbm, plan_ref, acc_ref,
    cur_buf, wh_ref, wl_ref, tw_ref, fine_ref, coarse_ref, turned_ref, mid_ref, map_ref, off_ref, in_sems,
    *, sections, batch
):
    depths, _, rows, width = cur_ref.shape
    padded = 2 * width
    inner = padded // RADIX
    taps = width // RADIX
    tall = batch * rows
    groups = depths // batch

    def load(g):
        return pltpu.make_async_copy(
            cur_ref.at[pl.ds(g * batch, batch)], cur_buf.at[pl.ds(g * batch, batch)], in_sems.at[g]
        )

    load(0).start()
    pairs = [
        (map_hbm, map_ref), (off_hbm, off_ref), (wh_hbm, wh_ref), (wl_hbm, wl_ref),
        (tw_hbm, tw_ref), (coarse_hbm, coarse_ref), (fine_hbm, fine_ref),
    ]
    entering = copy_all([
        pltpu.make_async_copy(source, target, in_sems.at[groups + i])
        for i, (source, target) in enumerate(pairs)
    ])
    scalars_in, weights_in, turns_in = entering[:2], entering[2:4], entering[4:]
    for g in range(1, groups):
        load(g).start()
    acc_ref[...] = jnp.zeros(acc_ref.shape, F32)
    wait_all(scalars_in)
    make_plan(map_ref, plan_ref, depths=depths, sections=sections)

    @pl.loop(0, groups)
    def _(g):
        load(g).wait()
        for c in range(2):
            turned_ref[c] = cur_buf[pl.ds(g * batch, batch), c].reshape(tall, width).T
        pieces = []
        for r in range(RADIX):
            pieces.append(
                jnp.concatenate(
                    [turned_ref[c, pl.ds(r, taps, stride=RADIX), :].T for c in range(2)], axis=1
                )
            )

        @pl.when(g == 0)
        def _():
            wait_all(weights_in)

        mid_ref[...] = dot3(jnp.concatenate(pieces, axis=0), wh_ref[...], wl_ref[...])

        @pl.when(g == 0)
        def _():
            wait_all(turns_in)

        @pl.loop(0, batch)
        def _(jj):
            j = g * batch + jj
            turn = phase_rows(fine_ref, coarse_ref, off_ref[j])
            slot = plan_ref[1 + sections + j]
            for k in range(0, inner, LANES):
                values = []
                for r in range(RADIX):
                    at = pl.ds(r * tall + jj * rows, rows)
                    value = tuple(mid_ref[at, d * inner + k : d * inner + k + LANES] for d in range(2))
                    if r > 0:
                        value = cmul(value, tuple(tw_ref[d, r : r + 1, k : k + LANES] for d in range(2)))
                    values.append(value)
                for q, value in enumerate(butterfly(values, -1.0)):
                    lanes = slice(q * inner + k, q * inner + k + LANES)
                    b = (q * inner + k) // LANES
                    value = cmul(value, (turn[0][b : b + 1], turn[1][b : b + 1]))
                    for d in range(2):
                        acc_ref[slot, d, :, lanes] += value[d]


def pack_kernel(acc_ref, *rest, slots, hops):
    parts = len(hops)
    outs = rest[:parts]
    stage_ref = rest[parts]
    _, _, rows, padded = acc_ref.shape
    me = lax.axis_index("lat")
    low = lax.broadcasted_iota(jnp.int32, (rows, LANES), 1) < LANES // 2

    @pl.loop(0, slots)
    def _(u):
        for b in range(padded // LANES):
            lanes = slice(b * LANES, (b + 1) * LANES)
            even, odd = trade_halves(acc_ref[u, 0, :, lanes], acc_ref[u, 1, :, lanes], low)
            stage_ref[u, 2 * b] = even
            stage_ref[u, 2 * b + 1] = odd

    @pl.loop(0, slots)
    def _(u):
        for out_ref, d in zip(outs, hops):
            out_ref[u] = stage_ref[u, me ^ d]


def couple_kernel(plan_ref, *rest, slots, hops):
    parts = len(hops)
    ins = rest[:parts]
    wh_ref, wl_ref, vh_ref, vl_ref, tw_ref, green_ref = rest[parts : parts + 6]
    outs = rest[parts + 6 : 2 * parts + 6]
    (order_buf, green_buf, spec_ref, mid_ref, lhs_ref, sems) = rest[2 * parts + 6 :]
    rows = ins[0].shape[1]
    columns, padded = green_buf.shape[3], green_buf.shape[4]
    inner = padded // RADIX
    taps = parts * rows // RADIX
    me = lax.axis_index("lat")

    def place(d):
        return pl.ds(pl.multiple_of((me ^ d) * rows, rows), rows)

    def fetch(t, s):
        return pltpu.make_async_copy(
            green_ref.at[plan_ref[1 + t], plan_ref[1 + s]], green_buf.at[t, s], sems.at[t, s]
        )

    @pl.loop(0, slots)
    def _(t):
        for s in range(slots):
            fetch(t, s).start()

    def transform(first, count):
        blocks = []
        for i in range(count):
            for in_ref, d in zip(ins, hops):
                order_buf[i, place(d), :] = in_ref[first + i]
            for r in range(RADIX):
                tall = order_buf[i, pl.ds(r, taps, stride=RADIX), :].T
                blocks.append(jnp.concatenate([tall[:columns], tall[columns:]], axis=1))
        mid_ref[: count * RADIX * columns] = dot3(jnp.concatenate(blocks, axis=0), wh_ref[...], wl_ref[...])

        @pl.loop(0, columns // 16)
        def _(a16):
            for i in range(count):
                for k in range(0, inner, LANES):
                    values = []
                    for r in range(RADIX):
                        at = pl.ds(pl.multiple_of((i * RADIX + r) * columns + a16 * 16, 16), 16)
                        value = tuple(mid_ref[at, d * inner + k : d * inner + k + LANES] for d in range(2))
                        if r > 0:
                            value = cmul(value, tuple(tw_ref[d, r : r + 1, k : k + LANES] for d in range(2)))
                        values.append(value)
                    for q, value in enumerate(butterfly(values, -1.0)):
                        at = pl.ds(pl.multiple_of(a16 * 16, 16), 16)
                        for d in range(2):
                            spec_ref[first + i, d, at, q * inner + k : q * inner + k + LANES] = value[d]

    @pl.loop(0, slots // 2)
    def _(pair):
        transform(2 * pair, 2)

    if slots % 2:
        transform(slots - 1, 1)

    def receive(first, count):
        for i in range(count):
            for s in range(slots):
                fetch(first + i, s).wait()

        @pl.loop(0, columns // 8)
        def _(a8):
            at = pl.ds(pl.multiple_of(a8 * 8, 8), 8)
            for k in range(0, inner, LANES):
                coupled = [[] for _ in range(count)]
                for q in range(RADIX):
                    lanes = slice(q * inner + k, q * inner + k + LANES)
                    totals = [None] * count
                    for s in range(slots):
                        source = tuple(spec_ref[s, d, at, lanes] for d in range(2))
                        for i in range(count):
                            factor = tuple(green_buf[first + i, s, d, at, lanes] for d in range(2))
                            term = cmul(factor, source)
                            totals[i] = term if totals[i] is None else cadd(totals[i], term)
                    for i in range(count):
                        coupled[i].append(totals[i])
                for i in range(count):
                    for r, value in enumerate(butterfly(coupled[i], 1.0)):
                        if r > 0:
                            back = (tw_ref[0, r : r + 1, k : k + LANES], -tw_ref[1, r : r + 1, k : k + LANES])
                            value = cmul(value, back)
                        for d in range(2):
                            here = pl.ds(pl.multiple_of((i * RADIX + r) * columns + a8 * 8, 8), 8)
                            lhs_ref[here, d * inner + k : d * inner + k + LANES] = value[d]

        result = dot3(lhs_ref[: count * RADIX * columns], vh_ref[...], vl_ref[...])
        for i in range(count):
            for r in range(RADIX):
                block = result[(i * RADIX + r) * columns : (i * RADIX + r + 1) * columns]
                tall = jnp.concatenate([block[:, :taps], block[:, taps:]], axis=0).T
                order_buf[i, pl.ds(r, taps, stride=RADIX), :] = tall
            for out_ref, d in zip(outs, hops):
                out_ref[first + i] = order_buf[i, place(d), :]

    @pl.loop(0, slots // 2)
    def _(pair):
        receive(2 * pair, 2)

    if slots % 2:
        receive(slots - 1, 1)


def fields_kernel(plan_ref, off_ref, *rest, slots, sections, batch, hops):
    parts = len(hops)
    ins = rest[:parts]
    vh_ref, vl_ref, tw_ref, fine_ref, coarse_ref, out_hbm = rest[parts : parts + 6]
    out_ref, spec_ref, lhs_ref, turned_ref, stage_ref, out_sems = rest[parts + 6 :]
    depths, _, rows, width = out_ref.shape
    padded = 2 * width
    inner = padded // RADIX
    taps = width // RADIX
    tall = batch * rows
    groups = depths // batch
    low = lax.broadcasted_iota(jnp.int32, (rows, LANES), 1) < LANES // 2
    me = lax.axis_index("lat")

    def store(g):
        at = pl.ds(g * batch, batch)
        return pltpu.make_async_copy(out_ref.at[at], out_hbm.at[at], out_sems.at[g])

    @pl.loop(0, slots)
    def _(u):
        for in_ref, d in zip(ins, hops):
            stage_ref[u, me ^ d] = in_ref[u]

    @pl.loop(0, slots)
    def _(u):
        for b in range(padded // LANES):
            lanes = slice(b * LANES, (b + 1) * LANES)
            re, im = trade_halves(stage_ref[u, 2 * b], stage_ref[u, 2 * b + 1], low)
            spec_ref[u, 0, :, lanes] = re
            spec_ref[u, 1, :, lanes] = im

    @pl.loop(0, groups)
    def _(g):
        @pl.loop(0, batch)
        def _(jj):
            j = g * batch + jj
            turn = phase_rows(fine_ref, coarse_ref, off_ref[j])
            slot = plan_ref[1 + sections + j]
            for k in range(0, inner, LANES):
                values = []
                for q in range(RADIX):
                    lanes = slice(q * inner + k, q * inner + k + LANES)
                    b = (q * inner + k) // LANES
                    value = tuple(spec_ref[slot, d, :, lanes] for d in range(2))
                    values.append(cmul(value, (turn[0][b : b + 1], -turn[1][b : b + 1])))
                for r, value in enumerate(butterfly(values, 1.0)):
                    if r > 0:
                        back = (tw_ref[0, r : r + 1, k : k + LANES], -tw_ref[1, r : r + 1, k : k + LANES])
                        value = cmul(value, back)
                    for d in range(2):
                        here = pl.ds(r * tall + jj * rows, rows)
                        lhs_ref[here, d * inner + k : d * inner + k + LANES] = value[d]

        result = dot3(lhs_ref[...], vh_ref[...], vl_ref[...])
        for d in range(2):
            for r in range(RADIX):
                block = result[r * tall : (r + 1) * tall, d * taps : (d + 1) * taps]
                turned_ref[d, pl.ds(r, taps, stride=RADIX), :] = block.T
            out_ref[pl.ds(g * batch, batch), d] = turned_ref[d].T.reshape(batch, rows, width)
        store(g).start()

    for g in range(groups):
        store(g).wait()


def vmem():
    return pl.BlockSpec(memory_space=pltpu.VMEM)


def anywhere():
    return pl.BlockSpec(memory_space=pl.ANY)


def smem():
    return pl.BlockSpec(memory_space=pltpu.SMEM)


def params(scratch, spare):
    held = sum(math.prod(a.shape) * jnp.dtype(a.dtype).itemsize for a in scratch)
    return pltpu.CompilerParams(vmem_limit_bytes=held + spare * 1024 * 1024)


def per_device(currents, green, section_map, offsets, *, parts):
    depths, _, rows, width = currents.shape
    sections = green.shape[0]
    columns = green.shape[3]
    padded = 2 * width
    inner = padded // RADIX
    taps = width // RADIX
    batch = LANES // rows
    hops = hop_order(parts)
    (wh, wl), (vh, vl), twiddle, fine, coarse = (
        jax.tree.map(jnp.asarray, entry) for entry in tables(width)
    )
    groups = depths // batch
    dma = pltpu.SemaphoreType.DMA
    most = min(depths, sections)
    room = [
        pltpu.VMEM(currents.shape, F32),
        pltpu.VMEM(wh.shape, BF16),
        pltpu.VMEM(wl.shape, BF16),
        pltpu.VMEM(twiddle.shape, F32),
        pltpu.VMEM(fine.shape, F32),
        pltpu.VMEM(coarse.shape, F32),
        pltpu.VMEM((2, width, LANES), F32),
        pltpu.VMEM((RADIX * LANES, 2 * inner), F32),
    ]
    in_hbm = functools.partial(pltpu.with_memory_space_constraint, memory_space=pltpu.HBM)
    plan, acc = pl.pallas_call(
        functools.partial(rows_kernel, sections=sections, batch=batch),
        out_shape=[
            jax.ShapeDtypeStruct((1 + sections + depths,), jnp.int32),
            pltpu.VMEM((most, 2, rows, padded), F32),
        ],
        in_specs=[anywhere()] * 8,
        out_specs=[smem(), vmem()],
        scratch_shapes=room + [
            pltpu.SMEM(section_map.shape, jnp.int32),
            pltpu.SMEM(offsets.shape, jnp.int32),
            dma((groups + 7,)),
        ],
        compiler_params=params(room, 10),
        name="rows",
    )(in_hbm(section_map), in_hbm(offsets), in_hbm(currents), wh, wl, twiddle, fine, coarse)

    def exchange(sent):
        moved = [
            lax.ppermute(block, "lat", [(i, i ^ d) for i in range(parts)])
            for block, d in zip(sent[1:], hops[1:])
        ]
        return [sent[0], *moved]

    def run(slots, plan, acc, offsets, green, wh, wl, vh, vl, twiddle, fine, coarse):
        blocks = [jax.ShapeDtypeStruct((slots, rows, LANES), F32)] * parts
        room = [pltpu.VMEM((slots, parts, rows, LANES), F32)]
        sent = pl.pallas_call(
            functools.partial(pack_kernel, slots=slots, hops=hops),
            out_shape=blocks,
            in_specs=[vmem()],
            out_specs=[vmem()] * parts,
            scratch_shapes=room,
            compiler_params=params(room, 4),
            name=f"pack_{slots}",
        )(acc)
        got = exchange(sent)
        room = [
            pltpu.VMEM((2, width, LANES), F32),
            pltpu.VMEM((slots, slots, 2, columns, padded), F32),
            pltpu.VMEM((slots, 2, columns, padded), F32),
            pltpu.VMEM((2 * RADIX * columns, 2 * inner), F32),
            pltpu.VMEM((2 * RADIX * columns, 2 * inner), F32),
        ]
        back = pl.pallas_call(
            functools.partial(couple_kernel, slots=slots, hops=hops),
            out_shape=blocks,
            in_specs=[smem()] + [vmem()] * (parts + 5) + [anywhere()],
            out_specs=[vmem()] * parts,
            scratch_shapes=room + [dma((slots, slots))],
            compiler_params=params(room, 10),
            name=f"couple_{slots}",
        )(plan, *got, wh, wl, vh, vl, twiddle, green)
        home = exchange(back)
        room = [
            pltpu.VMEM(currents.shape, F32),
            pltpu.VMEM((slots, 2, rows, padded), F32),
            pltpu.VMEM((RADIX * LANES, 2 * inner), F32),
            pltpu.VMEM((2, width, LANES), F32),
            pltpu.VMEM((slots, parts, rows, LANES), F32),
        ]
        return pl.pallas_call(
            functools.partial(fields_kernel, slots=slots, sections=sections, batch=batch, hops=hops),
            out_shape=pltpu.HBM(currents.shape, F32),
            in_specs=[smem(), smem()] + [vmem()] * (parts + 5),
            out_specs=anywhere(),
            scratch_shapes=room + [dma((groups,))],
            compiler_params=params(room, 10),
            name=f"fields_{slots}",
        )(plan, offsets, *home, vh, vl, twiddle, fine, coarse)

    least = max(1, (most + 1) // 2 + 1)
    choices = list(range(least, most + 1))
    return lax.switch(
        jnp.maximum(plan[0] - least, 0),
        [functools.partial(run, slots) for slots in choices],
        plan, acc, offsets, green, wh, wl, vh, vl, twiddle, fine, coarse,
    )


def solution(mesh):
    parts = mesh.shape["lat"]

    def body(currents, green, section_map, offsets):
        depths, _, rows, width = currents.shape
        columns = green.shape[3]
        fits = (
            2 * columns == LANES
            and rows % (8 * RADIX) == 0
            and LANES % rows == 0
            and depths % (LANES // rows) == 0
            and width % (RADIX * LANES) == 0
            and columns * parts == 2 * width
            and parts & (parts - 1) == 0
        )
        if fits:
            return per_device(currents, green, section_map, offsets, parts=parts)
        return plain_per_device(currents, green, section_map, offsets)

    in_specs = (
        P("group", None, "lat", None),
        P("group", None, None, "lat", None),
        P("group"),
        P("group"),
    )
    out_specs = P("group", None, "lat", None)
    return jax.shard_map(
        body, mesh=mesh, in_specs=in_specs, out_specs=out_specs, check_vma=False
    )
```

```python
import functools
import math

import jax
import jax.numpy as jnp
import numpy as np
from jax import lax
from jax.experimental import pallas as pl
from jax.experimental.pallas import tpu as pltpu
from jax.sharding import PartitionSpec as P

RADIX = 4
LANES = 128
FINE = 32
F32 = jnp.float32
BF16 = jnp.bfloat16


def dft_table(n_in, n_out, period, sign_value):
    row_ids = lax.iota(jnp.int32, n_in)
    col_ids = lax.iota(jnp.int32, n_out)
    angles = (
        2.0 * math.pi / period * (row_ids[:, None] * col_ids[None, :] % period).astype(jnp.float32)
    )
    cosine = jnp.cos(angles)
    sine_part = sign_value * jnp.sin(angles)
    return jnp.stack(
        [jnp.stack([cosine, sine_part], axis=1), jnp.stack([-sine_part, cosine], axis=1)], axis=0
    )


def phases(offsets, period, sign_value):
    col_ids = lax.iota(jnp.int32, period)
    angles = (
        2.0 * math.pi / period * (offsets[:, None] * col_ids[None, :] % period).astype(jnp.float32)
    )
    return (jnp.cos(angles)[:, None, :], sign_value * jnp.sin(angles)[:, None, :])


def rotate(planes, cosine, sine_part):
    real_part = planes[:, 0] * cosine - planes[:, 1] * sine_part
    imag_part = planes[:, 0] * sine_part + planes[:, 1] * cosine
    return jnp.stack([real_part, imag_part], axis=1)


def plain_per_device(currents, green, section_map, offsets):
    highest = lax.Precision.HIGHEST
    plane_width = currents.shape[3]
    padded = 2 * plane_width
    sections = green.shape[0]
    forward = dft_table(plane_width, padded, padded, -1.0)
    inverse = dft_table(padded, plane_width, padded, 1.0)
    onehot = (section_map[:, None] == lax.iota(jnp.int32, sections)[None, :]).astype(jnp.float32)
    spec_y = jnp.einsum("jcxy,cydk->jdxk", currents, forward, precision=highest)
    cos_fwd, sin_fwd = phases(offsets, padded, -1.0)
    shifted = jnp.transpose(rotate(spec_y, cos_fwd, sin_fwd), (0, 2, 1, 3))
    grouped = jnp.einsum("js,jxdk->sxdk", onehot, shifted, precision=highest)
    spectra = jnp.einsum(
        "mxcq,cxdk->mdqk",
        lax.all_to_all(grouped, "lat", split_axis=3, concat_axis=1, tiled=True),
        forward,
        precision=highest,
    )
    green_real = green[:, :, 0]
    green_imag = green[:, :, 1]
    out_real = jnp.einsum(
        "tsqk,sqk->tqk", green_real, spectra[:, 0], precision=highest
    ) - jnp.einsum("tsqk,sqk->tqk", green_imag, spectra[:, 1], precision=highest)
    out_imag = jnp.einsum(
        "tsqk,sqk->tqk", green_real, spectra[:, 1], precision=highest
    ) + jnp.einsum("tsqk,sqk->tqk", green_imag, spectra[:, 0], precision=highest)
    coupled = jnp.stack([out_real, out_imag], axis=1)
    returned = lax.all_to_all(
        jnp.einsum("mcqk,ckdx->mdxq", coupled, inverse, precision=highest),
        "lat",
        split_axis=2,
        concat_axis=3,
        tiled=True,
    )
    per_depth = jnp.einsum("js,sdxq->jdxq", onehot, returned, precision=highest)
    cos_back, sin_back = phases(offsets, padded, 1.0)
    turned = rotate(per_depth, cos_back, sin_back)
    result = jnp.einsum("jcxk,ckdy->jdxy", turned, inverse, precision=highest)
    return result * (1.0 / (padded * padded))


def split_np(table):
    high = table.astype(BF16)
    low = (table - high.astype(np.float64)).astype(BF16)
    return high, low


def unit(products, period):
    angles = (2.0 * math.pi / period) * (products % period).astype(np.float64)
    return np.cos(angles), np.sin(angles)


def tables(width):
    padded = 2 * width
    inner = padded // RADIX
    taps = width // RADIX
    cosine, sine = unit(np.arange(taps)[:, None] * np.arange(inner)[None, :], inner)
    weights = np.concatenate(
        [np.concatenate([cosine, -sine], axis=1), np.concatenate([sine, cosine], axis=1)], axis=0
    )
    forward = split_np(weights)
    inverse = split_np(np.ascontiguousarray(weights.T) / (padded * 1.0))
    cosine, sine = unit(np.arange(8)[:, None] * np.arange(inner)[None, :], padded)
    twiddle = np.stack([cosine, -sine]).astype(np.float32)
    lanes = np.arange(padded).reshape(1, padded // LANES, LANES)
    cosine, sine = unit(np.arange(FINE)[:, None, None] * lanes, padded)
    fine = np.stack([cosine, -sine]).astype(np.float32)
    cosine, sine = unit(FINE * np.arange(width // FINE + 1)[:, None, None] * lanes[:, :1], padded)
    coarse = np.stack([cosine, -sine]).astype(np.float32)
    return forward, inverse, twiddle, fine, coarse


def cmul(a, b):
    return a[0] * b[0] - a[1] * b[1], a[0] * b[1] + a[1] * b[0]


def cadd(a, b):
    return a[0] + b[0], a[1] + b[1]


def csub(a, b):
    return a[0] - b[0], a[1] - b[1]


def butterfly(v, turn):
    even, odd = cadd(v[0], v[2]), csub(v[0], v[2])
    cross, diff = cadd(v[1], v[3]), csub(v[1], v[3])
    spun = (-turn * diff[1], turn * diff[0])
    return cadd(even, cross), cadd(odd, spun), csub(even, cross), csub(odd, spun)


def split(value):
    high = value.astype(BF16)
    return high, (value - high.astype(F32)).astype(BF16)


def dot3(value, high_table, low_table):
    high, low = split(value)
    dot = functools.partial(jnp.dot, preferred_element_type=F32)
    return dot(high, high_table) + (dot(high, low_table) + dot(low, high_table))


def phase_rows(fine_ref, coarse_ref, offset):
    fine_id = offset % FINE
    coarse_id = offset // FINE
    return cmul(
        tuple(fine_ref[d, fine_id] for d in range(2)),
        tuple(coarse_ref[d, coarse_id] for d in range(2)),
    )


def make_plan(map_ref, plan_ref, *, depths, sections):
    count = jnp.int32(0)
    for u in range(sections):
        plan_ref[1 + u] = jnp.int32(0)
    ids = [map_ref[j] for j in range(depths)]
    for s in range(sections):
        used = jnp.int32(0)
        for j in range(depths):
            used = jnp.maximum(used, (ids[j] == s).astype(jnp.int32))

        @pl.when(used > 0)
        def _(s=s, count=count):
            plan_ref[1 + count] = jnp.int32(s)
            for j in range(depths):
                @pl.when(ids[j] == s)
                def _(j=j):
                    plan_ref[1 + sections + j] = count

        count = count + used
    plan_ref[0] = count


def trade_halves(x, y, low):
    kept = jnp.where(low, x, y)
    moved = pltpu.roll(jnp.where(low, y, x), LANES // 2, 1)
    return jnp.where(low, kept, moved), jnp.where(low, moved, kept)


def hop_order(parts):
    quarter = max(parts // 4, 1)
    far = [d for low in range(quarter) for d in (2 * quarter + low, 3 * quarter + low) if d < parts]
    near = [d for d in range(quarter, 2 * quarter)] + [d for d in range(quarter - 1, 0, -1)]
    return (0, *far[:4], *near[:1], *far[4:], *near[1:])


def copy_all(copies):
    for copy in copies:
        copy.start()
    return copies


def wait_all(copies):
    for copy in copies:
        copy.wait()


def rows_kernel(
    map_hbm, off_hbm, cur_ref, wh_hbm, wl_hbm, tw_hbm, fine_hbm, coarse_hbm, plan_ref, acc_ref,
    cur_buf, wh_ref, wl_ref, tw_ref, fine_ref, coarse_ref, turned_ref, mid_ref, map_ref, off_ref, in_sems,
    *, sections, batch
):
    depths, _, rows, width = cur_ref.shape
    padded = 2 * width
    inner = padded // RADIX
    taps = width // RADIX
    tall = batch * rows
    groups = depths // batch

    def load(g):
        return pltpu.make_async_copy(
            cur_ref.at[pl.ds(g * batch, batch)], cur_buf.at[pl.ds(g * batch, batch)], in_sems.at[g]
        )

    load(0).start()
    pairs = [
        (map_hbm, map_ref), (off_hbm, off_ref), (wh_hbm, wh_ref), (wl_hbm, wl_ref),
        (tw_hbm, tw_ref), (coarse_hbm, coarse_ref), (fine_hbm, fine_ref),
    ]
    entering = copy_all([
        pltpu.make_async_copy(source, target, in_sems.at[groups + i])
        for i, (source, target) in enumerate(pairs)
    ])
    scalars_in, weights_in, turns_in = entering[:2], entering[2:4], entering[4:]
    for g in range(1, groups):
        load(g).start()
    acc_ref[...] = jnp.zeros(acc_ref.shape, F32)
    wait_all(scalars_in)
    make_plan(map_ref, plan_ref, depths=depths, sections=sections)

    @pl.loop(0, groups)
    def _(g):
        load(g).wait()
        for c in range(2):
            turned_ref[c] = cur_buf[pl.ds(g * batch, batch), c].reshape(tall, width).T
        pieces = []
        for r in range(RADIX):
            pieces.append(
                jnp.concatenate(
                    [turned_ref[c, pl.ds(r, taps, stride=RADIX), :].T for c in range(2)], axis=1
                )
            )

        @pl.when(g == 0)
        def _():
            wait_all(weights_in)

        mid_ref[...] = dot3(jnp.concatenate(pieces, axis=0), wh_ref[...], wl_ref[...])

        @pl.when(g == 0)
        def _():
            wait_all(turns_in)

        @pl.loop(0, batch)
        def _(jj):
            j = g * batch + jj
            turn = phase_rows(fine_ref, coarse_ref, off_ref[j])
            slot = plan_ref[1 + sections + j]
            for k in range(0, inner, LANES):
                values = []
                for r in range(RADIX):
                    at = pl.ds(r * tall + jj * rows, rows)
                    value = tuple(mid_ref[at, d * inner + k : d * inner + k + LANES] for d in range(2))
                    if r > 0:
                        value = cmul(value, tuple(tw_ref[d, r : r + 1, k : k + LANES] for d in range(2)))
                    values.append(value)
                for q, value in enumerate(butterfly(values, -1.0)):
                    lanes = slice(q * inner + k, q * inner + k + LANES)
                    b = (q * inner + k) // LANES
                    value = cmul(value, (turn[0][b : b + 1], turn[1][b : b + 1]))
                    for d in range(2):
                        acc_ref[slot, d, :, lanes] += value[d]


def pack_kernel(acc_ref, *rest, slots, hops):
    parts = len(hops)
    outs = rest[:parts]
    stage_ref = rest[parts]
    _, _, rows, padded = acc_ref.shape
    me = lax.axis_index("lat")
    low = lax.broadcasted_iota(jnp.int32, (rows, LANES), 1) < LANES // 2

    @pl.loop(0, slots)
    def _(u):
        for b in range(padded // LANES):
            lanes = slice(b * LANES, (b + 1) * LANES)
            even, odd = trade_halves(acc_ref[u, 0, :, lanes], acc_ref[u, 1, :, lanes], low)
            stage_ref[u, 2 * b] = even
            stage_ref[u, 2 * b + 1] = odd

    @pl.loop(0, slots)
    def _(u):
        for out_ref, d in zip(outs, hops):
            out_ref[u] = stage_ref[u, me ^ d]


def couple_kernel(plan_ref, *rest, slots, hops):
    parts = len(hops)
    ins = rest[:parts]
    wh_ref, wl_ref, vh_ref, vl_ref, tw_ref, green_ref = rest[parts : parts + 6]
    outs = rest[parts + 6 : 2 * parts + 6]
    (order_buf, green_buf, spec_ref, mid_ref, lhs_ref, sems) = rest[2 * parts + 6 :]
    rows = ins[0].shape[1]
    columns, padded = green_buf.shape[3], green_buf.shape[4]
    inner = padded // RADIX
    taps = parts * rows // RADIX
    me = lax.axis_index("lat")

    def place(d):
        return pl.ds(pl.multiple_of((me ^ d) * rows, rows), rows)

    def fetch(t, s):
        return pltpu.make_async_copy(
            green_ref.at[plan_ref[1 + t], plan_ref[1 + s]], green_buf.at[t, s], sems.at[t, s]
        )

    def request(t):
        for s in range(slots):
            fetch(t, s).start()

    for t in range(min(2, slots)):
        request(t)

    def transform(first, count):
        blocks = []
        for i in range(count):
            for in_ref, d in zip(ins, hops):
                order_buf[i, place(d), :] = in_ref[first + i]
            for r in range(RADIX):
                tall = order_buf[i, pl.ds(r, taps, stride=RADIX), :].T
                blocks.append(jnp.concatenate([tall[:columns], tall[columns:]], axis=1))
        mid_ref[: count * RADIX * columns] = dot3(jnp.concatenate(blocks, axis=0), wh_ref[...], wl_ref[...])

        @pl.loop(0, columns // 16)
        def _(a16):
            for i in range(count):
                for k in range(0, inner, LANES):
                    values = []
                    for r in range(RADIX):
                        at = pl.ds(pl.multiple_of((i * RADIX + r) * columns + a16 * 16, 16), 16)
                        value = tuple(mid_ref[at, d * inner + k : d * inner + k + LANES] for d in range(2))
                        if r > 0:
                            value = cmul(value, tuple(tw_ref[d, r : r + 1, k : k + LANES] for d in range(2)))
                        values.append(value)
                    for q, value in enumerate(butterfly(values, -1.0)):
                        at = pl.ds(pl.multiple_of(a16 * 16, 16), 16)
                        for d in range(2):
                            spec_ref[first + i, d, at, q * inner + k : q * inner + k + LANES] = value[d]

    @pl.loop(0, slots // 2)
    def _(pair):
        for i in range(2):
            @pl.when(2 * pair + 2 + i < slots)
            def _(i=i):
                request(2 * pair + 2 + i)

        transform(2 * pair, 2)

    if slots % 2:
        transform(slots - 1, 1)

    def receive(first, count):
        for i in range(count):
            for s in range(slots):
                fetch(first + i, s).wait()

        @pl.loop(0, columns // 8)
        def _(a8):
            at = pl.ds(pl.multiple_of(a8 * 8, 8), 8)
            for k in range(0, inner, LANES):
                coupled = [[] for _ in range(count)]
                for q in range(RADIX):
                    lanes = slice(q * inner + k, q * inner + k + LANES)
                    totals = [None] * count
                    for s in range(slots):
                        source = tuple(spec_ref[s, d, at, lanes] for d in range(2))
                        for i in range(count):
                            factor = tuple(green_buf[first + i, s, d, at, lanes] for d in range(2))
                            term = cmul(factor, source)
                            totals[i] = term if totals[i] is None else cadd(totals[i], term)
                    for i in range(count):
                        coupled[i].append(totals[i])
                for i in range(count):
                    for r, value in enumerate(butterfly(coupled[i], 1.0)):
                        if r > 0:
                            back = (tw_ref[0, r : r + 1, k : k + LANES], -tw_ref[1, r : r + 1, k : k + LANES])
                            value = cmul(value, back)
                        for d in range(2):
                            here = pl.ds(pl.multiple_of((i * RADIX + r) * columns + a8 * 8, 8), 8)
                            lhs_ref[here, d * inner + k : d * inner + k + LANES] = value[d]

        result = dot3(lhs_ref[: count * RADIX * columns], vh_ref[...], vl_ref[...])
        for i in range(count):
            for r in range(RADIX):
                block = result[(i * RADIX + r) * columns : (i * RADIX + r + 1) * columns]
                tall = jnp.concatenate([block[:, :taps], block[:, taps:]], axis=0).T
                order_buf[i, pl.ds(r, taps, stride=RADIX), :] = tall
            for out_ref, d in zip(outs, hops):
                out_ref[first + i] = order_buf[i, place(d), :]

    @pl.loop(0, slots // 2)
    def _(pair):
        receive(2 * pair, 2)

    if slots % 2:
        receive(slots - 1, 1)


def fields_kernel(plan_ref, off_ref, *rest, slots, sections, batch, hops):
    parts = len(hops)
    ins = rest[:parts]
    vh_ref, vl_ref, tw_ref, fine_ref, coarse_ref, out_hbm = rest[parts : parts + 6]
    out_ref, spec_ref, lhs_ref, turned_ref, stage_ref, out_sems = rest[parts + 6 :]
    depths, _, rows, width = out_ref.shape
    padded = 2 * width
    inner = padded // RADIX
    taps = width // RADIX
    tall = batch * rows
    groups = depths // batch
    low = lax.broadcasted_iota(jnp.int32, (rows, LANES), 1) < LANES // 2
    me = lax.axis_index("lat")

    def store(g):
        at = pl.ds(g * batch, batch)
        return pltpu.make_async_copy(out_ref.at[at], out_hbm.at[at], out_sems.at[g])

    @pl.loop(0, slots)
    def _(u):
        for in_ref, d in zip(ins, hops):
            stage_ref[u, me ^ d] = in_ref[u]

    @pl.loop(0, slots)
    def _(u):
        for b in range(padded // LANES):
            lanes = slice(b * LANES, (b + 1) * LANES)
            re, im = trade_halves(stage_ref[u, 2 * b], stage_ref[u, 2 * b + 1], low)
            spec_ref[u, 0, :, lanes] = re
            spec_ref[u, 1, :, lanes] = im

    @pl.loop(0, groups)
    def _(g):
        @pl.loop(0, batch)
        def _(jj):
            j = g * batch + jj
            turn = phase_rows(fine_ref, coarse_ref, off_ref[j])
            slot = plan_ref[1 + sections + j]
            for k in range(0, inner, LANES):
                values = []
                for q in range(RADIX):
                    lanes = slice(q * inner + k, q * inner + k + LANES)
                    b = (q * inner + k) // LANES
                    value = tuple(spec_ref[slot, d, :, lanes] for d in range(2))
                    values.append(cmul(value, (turn[0][b : b + 1], -turn[1][b : b + 1])))
                for r, value in enumerate(butterfly(values, 1.0)):
                    if r > 0:
                        back = (tw_ref[0, r : r + 1, k : k + LANES], -tw_ref[1, r : r + 1, k : k + LANES])
                        value = cmul(value, back)
                    for d in range(2):
                        here = pl.ds(r * tall + jj * rows, rows)
                        lhs_ref[here, d * inner + k : d * inner + k + LANES] = value[d]

        result = dot3(lhs_ref[...], vh_ref[...], vl_ref[...])
        for d in range(2):
            for r in range(RADIX):
                block = result[r * tall : (r + 1) * tall, d * taps : (d + 1) * taps]
                turned_ref[d, pl.ds(r, taps, stride=RADIX), :] = block.T
            out_ref[pl.ds(g * batch, batch), d] = turned_ref[d].T.reshape(batch, rows, width)
        store(g).start()

    for g in range(groups):
        store(g).wait()


def vmem():
    return pl.BlockSpec(memory_space=pltpu.VMEM)


def anywhere():
    return pl.BlockSpec(memory_space=pl.ANY)


def smem():
    return pl.BlockSpec(memory_space=pltpu.SMEM)


def params(scratch, spare):
    held = sum(math.prod(a.shape) * jnp.dtype(a.dtype).itemsize for a in scratch)
    return pltpu.CompilerParams(vmem_limit_bytes=held + spare * 1024 * 1024)


def per_device(currents, green, section_map, offsets, *, parts):
    depths, _, rows, width = currents.shape
    sections = green.shape[0]
    columns = green.shape[3]
    padded = 2 * width
    inner = padded // RADIX
    taps = width // RADIX
    batch = LANES // rows
    hops = hop_order(parts)
    (wh, wl), (vh, vl), twiddle, fine, coarse = (
        jax.tree.map(jnp.asarray, entry) for entry in tables(width)
    )
    groups = depths // batch
    dma = pltpu.SemaphoreType.DMA
    most = min(depths, sections)
    room = [
        pltpu.VMEM(currents.shape, F32),
        pltpu.VMEM(wh.shape, BF16),
        pltpu.VMEM(wl.shape, BF16),
        pltpu.VMEM(twiddle.shape, F32),
        pltpu.VMEM(fine.shape, F32),
        pltpu.VMEM(coarse.shape, F32),
        pltpu.VMEM((2, width, LANES), F32),
        pltpu.VMEM((RADIX * LANES, 2 * inner), F32),
    ]
    in_hbm = functools.partial(pltpu.with_memory_space_constraint, memory_space=pltpu.HBM)
    plan, acc = pl.pallas_call(
        functools.partial(rows_kernel, sections=sections, batch=batch),
        out_shape=[
            jax.ShapeDtypeStruct((1 + sections + depths,), jnp.int32),
            pltpu.VMEM((most, 2, rows, padded), F32),
        ],
        in_specs=[anywhere()] * 8,
        out_specs=[smem(), vmem()],
        scratch_shapes=room + [
            pltpu.SMEM(section_map.shape, jnp.int32),
            pltpu.SMEM(offsets.shape, jnp.int32),
            dma((groups + 7,)),
        ],
        compiler_params=params(room, 10),
        name="rows",
    )(in_hbm(section_map), in_hbm(offsets), in_hbm(currents), wh, wl, twiddle, fine, coarse)

    def exchange(sent):
        moved = [
            lax.ppermute(block, "lat", [(i, i ^ d) for i in range(parts)])
            for block, d in zip(sent[1:], hops[1:])
        ]
        return [sent[0], *moved]

    def run(slots, plan, acc, offsets, green, wh, wl, vh, vl, twiddle, fine, coarse):
        blocks = [jax.ShapeDtypeStruct((slots, rows, LANES), F32)] * parts
        room = [pltpu.VMEM((slots, parts, rows, LANES), F32)]
        sent = pl.pallas_call(
            functools.partial(pack_kernel, slots=slots, hops=hops),
            out_shape=blocks,
            in_specs=[vmem()],
            out_specs=[vmem()] * parts,
            scratch_shapes=room,
            compiler_params=params(room, 4),
            name=f"pack_{slots}",
        )(acc)
        got = exchange(sent)
        room = [
            pltpu.VMEM((2, width, LANES), F32),
            pltpu.VMEM((slots, slots, 2, columns, padded), F32),
            pltpu.VMEM((slots, 2, columns, padded), F32),
            pltpu.VMEM((2 * RADIX * columns, 2 * inner), F32),
            pltpu.VMEM((2 * RADIX * columns, 2 * inner), F32),
        ]
        back = pl.pallas_call(
            functools.partial(couple_kernel, slots=slots, hops=hops),
            out_shape=blocks,
            in_specs=[smem()] + [vmem()] * (parts + 5) + [anywhere()],
            out_specs=[vmem()] * parts,
            scratch_shapes=room + [dma((slots, slots))],
            compiler_params=params(room, 10),
            name=f"couple_{slots}",
        )(plan, *got, wh, wl, vh, vl, twiddle, green)
        home = exchange(back)
        room = [
            pltpu.VMEM(currents.shape, F32),
            pltpu.VMEM((slots, 2, rows, padded), F32),
            pltpu.VMEM((RADIX * LANES, 2 * inner), F32),
            pltpu.VMEM((2, width, LANES), F32),
            pltpu.VMEM((slots, parts, rows, LANES), F32),
        ]
        return pl.pallas_call(
            functools.partial(fields_kernel, slots=slots, sections=sections, batch=batch, hops=hops),
            out_shape=pltpu.HBM(currents.shape, F32),
            in_specs=[smem(), smem()] + [vmem()] * (parts + 5),
            out_specs=anywhere(),
            scratch_shapes=room + [dma((groups,))],
            compiler_params=params(room, 10),
            name=f"fields_{slots}",
        )(plan, offsets, *home, vh, vl, twiddle, fine, coarse)

    least = max(1, (most + 1) // 2 + 1)
    choices = list(range(least, most + 1))
    return lax.switch(
        jnp.maximum(plan[0] - least, 0),
        [functools.partial(run, slots) for slots in choices],
        plan, acc, offsets, green, wh, wl, vh, vl, twiddle, fine, coarse,
    )


def solution(mesh):
    parts = mesh.shape["lat"]

    def body(currents, green, section_map, offsets):
        depths, _, rows, width = currents.shape
        columns = green.shape[3]
        fits = (
            2 * columns == LANES
            and rows % (8 * RADIX) == 0
            and LANES % rows == 0
            and depths % (LANES // rows) == 0
            and width % (RADIX * LANES) == 0
            and columns * parts == 2 * width
            and parts & (parts - 1) == 0
        )
        if fits:
            return per_device(currents, green, section_map, offsets, parts=parts)
        return plain_per_device(currents, green, section_map, offsets)

    in_specs = (
        P("group", None, "lat", None),
        P("group", None, None, "lat", None),
        P("group"),
        P("group"),
    )
    out_specs = P("group", None, "lat", None)
    return jax.shard_map(
        body, mesh=mesh, in_specs=in_specs, out_specs=out_specs, check_vma=False
    )
```
